32 devices in a mesh: runner: 4 (over z), cells: 8 (over y, x, core).
Axes of the slice: x: 2, y: 2, z: 4, core: 2. Of those that a mesh axis runs over, the one named last changes fastest.
Arguments:
- states: float32 [512, 64, 128], P('runner', 'cells'), may hold values from -4 to 4
- diffusivity: float32 [64, 128], P('cells'), may hold values from 0.03 to 0.2
- velocity: float32 [2, 64, 128], P(None, 'cells'), may hold values from -0.15 to 0.15
- counts: int32 [4], replicated, may hold values from 1 to 128, 256 in all
- obs_index: int32 [4096], P('cells'), may hold values from 0 to 1023
- obs_value: float32 [4096], P('cells'), may hold values from -6 to 6
- obs_weight: float32 [4096], P('cells'), may hold values from 0.3 to 3
Outputs:
- analysed: float32 [512, 64, 128], P('runner', 'cells')
The draws below stay inside these ranges and needn't reach their ends.
Inputs may be any that keep to these rules, and one draw needn't show every extreme that they name: Runner r's members fill its first counts[r] slots, in runner order; the counts sum to 256 and the largest is exactly 128. Observation k lies in the rows of cells index k // 512; obs_index counts cells within those 8 x 128 cells, row by row; a cell may be observed more than once.
All inputs are finite; a program needn't handle non-finite values.
Results may differ from the reference program's by a relative error of at most 0.013.
Values may be sent and summed in bfloat16 or wider, within the bound.
No kernel may reach another device: no remote copies, remote signals or barrier semaphores. Data moves between devices by JAX's collectives and lax.ppermute only.
A program may use at most 64 MiB of HBM per device.

```python
import math
import jax
import jax.numpy as jnp
import numpy as np
from jax import lax

CX = 8
GRID_COLUMNS = 128
OBS_DEV = 512
STEPS = 4
RUNNER_SLOTS = 128
MEMBER_COUNT = 256
GRID_ROWS = 64
NOBS = 4096
N_RUNNER = 4


def with_ends(result, stream_key, low, top_value):
    shape = result.shape
    index_at = [jax.random.randint(jax.random.fold_in(stream_key, axis), (), 0, shape[axis]) for axis in range(len(shape))]
    result = result.at[tuple(index_at)].set(low)
    longest = shape.index(max(shape))
    index_at[longest] = (index_at[longest] + 1) % shape[longest]
    return result.at[tuple(index_at)].set(top_value)


def block_scale(own_key, extent, split, smallest, high):
    loudness = 1.0
    for dim, shards_of in split:
        draws = jax.random.uniform(jax.random.fold_in(jax.random.fold_in(own_key, 6), dim), (shards_of,), jnp.float32, smallest / len(split), high / len(split))
        loudness = loudness * jnp.repeat(jnp.exp(draws), extent[dim] // shards_of).reshape((-1,) + (1,) * (len(extent) - 1 - dim))
    return loudness


def split_up(count, total, bound, lean):
    loads = [(1 << 20) // math.isqrt(standing ** lean) + 1 for standing in range(2, count + 1)]
    rest, given = total - bound - (count - 1), [1] * (count - 1)
    while rest > 0:
        movable = [i for i in range(count - 1) if given[i] < bound]
        pool, budget = sum([loads[i] for i in movable]), rest
        for i in movable:
            extra = min(bound - given[i], max(1, budget * loads[i] // pool), rest)
            given[i] = given[i] + extra
            rest = rest - extra
    return np.array([bound] + given)


def ragged_sizes(rng, number_of, total, limit, lean):
    if number_of == 2:
        one = jax.random.randint(rng, (), max(1, total - limit), min(limit, total - 1) + 1)
        return jnp.stack([one, total - one])
    lengths = jnp.asarray(split_up(number_of, total, limit, lean), jnp.int32)
    pairs = (number_of - 1) // 2
    giver, receiver = lengths[1:1 + 2 * pairs:2], lengths[2:2 + 2 * pairs:2]
    room = jnp.minimum(giver - 1, limit - receiver)
    moved = jax.random.randint(jax.random.fold_in(rng, 1), (pairs,), 0, 1 << 20) % (room + 1)
    lengths = lengths.at[1:1 + 2 * pairs:2].set(giver - moved).at[2:2 + 2 * pairs:2].set(receiver + moved)
    return lengths[jax.random.permutation(jax.random.fold_in(rng, 2), number_of)]


def gaussian(key, extent, spread, reach, shards=(), kind=jnp.bfloat16):
    entries = spread * jax.random.normal(key, extent, jnp.float32)
    if shards:
        entries = entries * block_scale(key, extent, shards, -0.22, 0.18)
    return jnp.clip(entries, -reach, reach).astype(kind)


def setup_inputs(seed: int = 0) -> dict:
    seeds = jax.random.split(jax.random.key(seed), 8)
    states = gaussian(seeds[0], (N_RUNNER * RUNNER_SLOTS, GRID_ROWS, GRID_COLUMNS), 0.7, 4.0, ((0, 4), (1, 8)), jnp.float32)
    diffusivity = jnp.clip(jnp.exp(math.log(0.2) - 1.89712 * jax.random.uniform(seeds[1], (GRID_ROWS, GRID_COLUMNS), jnp.float32) ** block_scale(seeds[1], (GRID_ROWS, GRID_COLUMNS), ((0, 8),), -0.2, 0.2)), 0.03, 0.2)
    velocity = jnp.clip(jax.random.uniform(seeds[2], (2, GRID_ROWS, GRID_COLUMNS), jnp.float32, -0.15, 0.15) * block_scale(seeds[2], (2, GRID_ROWS, GRID_COLUMNS), ((1, 8),), -0.4, 0.0), -0.15, 0.15)
    counts = ragged_sizes(seeds[3], N_RUNNER, MEMBER_COUNT, RUNNER_SLOTS, 2).astype(jnp.int32)
    obs_index = with_ends(jax.random.randint(seeds[4], (NOBS,), 0, CX * GRID_COLUMNS), jax.random.fold_in(seeds[4], 1), 0, (CX * GRID_COLUMNS) - 1).astype(jnp.int32)
    obs_value = gaussian(seeds[5], (NOBS,), 1.0, 6.0, ((0, 8),), jnp.float32)
    obs_weight = jnp.clip(jnp.exp(math.log(3.0) - 2.3025851 * jax.random.uniform(seeds[6], (NOBS,), jnp.float32) ** block_scale(seeds[6], (NOBS,), ((0, 8),), -0.2, 0.2)), 0.3, 3.0)
    return {"states": states, "diffusivity": diffusivity, "velocity": velocity, "counts": counts, "obs_index": obs_index, "obs_value": obs_value, "obs_weight": obs_weight}


def stencil(values, diffusivity, velocity):
    upper_row = jnp.roll(values, -1, axis=-2)
    lower_row = jnp.roll(values, 1, axis=-2)
    right_col = jnp.roll(values, -1, axis=-1)
    left_col = jnp.roll(values, 1, axis=-1)
    laplace = upper_row + lower_row + right_col + left_col - 4.0 * values
    return (values + diffusivity * laplace - 0.5 * velocity[0] * (upper_row - lower_row)
            - 0.5 * velocity[1] * (right_col - left_col) - 0.05 * values * values * values)


def reference(states, diffusivity, velocity, counts, obs_index, obs_value, obs_weight):
    worker_blocks = states.reshape(N_RUNNER, RUNNER_SLOTS, GRID_ROWS, GRID_COLUMNS)

    def march_forward(block_states):
        values = block_states
        for iteration in range(STEPS):
            values = stencil(values, diffusivity, velocity)
        return values

    predicted_states = lax.map(march_forward, worker_blocks).reshape(N_RUNNER * RUNNER_SLOTS, GRID_ROWS * GRID_COLUMNS)
    run_ends = jnp.cumsum(counts).astype(jnp.int32)
    offsets = (run_ends - counts).astype(jnp.int32)
    slot_ids = jnp.arange(RUNNER_SLOTS, dtype=jnp.int32)
    is_live = (slot_ids[None, :] < counts[:, None]).reshape(-1)
    member_ids = jnp.arange(MEMBER_COUNT, dtype=jnp.int32)
    owner_run = jnp.sum((run_ends[None, :] <= member_ids[:, None]).astype(jnp.int32), axis=1).astype(jnp.int32)
    slot_of = (owner_run * RUNNER_SLOTS + member_ids - offsets[owner_run]).astype(jnp.int32)
    active_mask = is_live.astype(jnp.float32)[:, None]
    ensemble_mean = jnp.sum(predicted_states * active_mask, axis=0) / MEMBER_COUNT
    member_deviation = ((predicted_states - ensemble_mean) * active_mask).astype(jnp.bfloat16)
    compact = member_deviation[slot_of]
    obs_cells = ((jnp.arange(NOBS, dtype=jnp.int32) // OBS_DEV) * (CX * GRID_COLUMNS) + obs_index).astype(jnp.int32)
    observed = compact[:, obs_cells]
    weighted = (observed.astype(jnp.float32) * obs_weight).astype(jnp.bfloat16)
    gram_full = jnp.dot(weighted, observed.T, preferred_element_type=jnp.float32)
    trace_sum = jnp.trace(gram_full)
    scaling = MEMBER_COUNT / trace_sum
    innovation = obs_value - ensemble_mean[obs_cells]
    bias_vector = (jnp.dot(weighted.astype(jnp.float32), innovation, precision=lax.Precision.HIGHEST) * scaling).astype(jnp.bfloat16)
    scaled = (gram_full * scaling).astype(jnp.bfloat16)
    square = jnp.dot(scaled, scaled, preferred_element_type=jnp.float32).astype(jnp.bfloat16)
    cubed = jnp.dot(square, scaled, preferred_element_type=jnp.float32)
    transform = (1.0 * jnp.eye(MEMBER_COUNT, dtype=jnp.float32) - 0.5 * scaled.astype(jnp.float32)
                 + 0.375 * square.astype(jnp.float32) - 0.3125 * cubed)
    shift_weights = jnp.dot(transform, bias_vector.astype(jnp.float32), precision=lax.Precision.HIGHEST)
    increment = jnp.dot(shift_weights, compact.astype(jnp.float32), precision=lax.Precision.HIGHEST)
    applied = jnp.dot(transform.astype(jnp.bfloat16), compact, preferred_element_type=jnp.float32)
    analysed = ensemble_mean + increment + applied
    slotted = jnp.zeros((N_RUNNER * RUNNER_SLOTS, GRID_ROWS * GRID_COLUMNS), jnp.float32).at[slot_of].set(analysed)
    return slotted.reshape(N_RUNNER * RUNNER_SLOTS, GRID_ROWS, GRID_COLUMNS)
```

```python
import functools

import jax
import jax.numpy as jnp
from jax import lax
from jax.experimental import pallas as pl
from jax.experimental.pallas import tpu as pltpu
from jax.sharding import PartitionSpec as P

STEPS = 4
PAD = 16
F32 = jnp.float32
BF16 = jnp.bfloat16


def partners(count, step):
    if count & (count - 1):
        return [(i, (i + step) % count) for i in range(count)]
    return [(i, i ^ step) for i in range(count)]


def source_of(count, step, rank):
    if count & (count - 1):
        return lax.rem(rank + (count - step), count)
    return rank ^ step


def pieces(row):
    high = row.astype(BF16).astype(F32)
    rest = row - high
    middle = rest.astype(BF16).astype(F32)
    return high, middle, rest - middle


def stacked(rows, height):
    width = rows[0].shape[1]
    place = lax.broadcasted_iota(jnp.int32, (height, width), 0)
    total = jnp.zeros((height, width), F32)
    for index, row in enumerate(rows):
        total = jnp.where(place == index, row, total)
    return total.astype(BF16)


def joined(block, first):
    block = block.astype(F32)
    return block[first : first + 1] + block[first + 1 : first + 2] + block[first + 2 : first + 3]


def offset_of(counts_ref, runner, runners):
    total = jnp.int32(0)
    for index in range(runners):
        total = total + jnp.where(index < runner, counts_ref[index], 0)
    return total


def call(kernel, out_shape, n_vector, n_scalar=0, flops=0, scratch=()):
    vector = pl.BlockSpec(memory_space=pltpu.VMEM)
    scalar = pl.BlockSpec(memory_space=pltpu.SMEM)
    many = isinstance(out_shape, (tuple, list))
    return pl.pallas_call(
        kernel,
        out_shape=out_shape,
        in_specs=[scalar] * n_scalar + [vector] * n_vector,
        out_specs=type(out_shape)([vector] * len(out_shape)) if many else vector,
        scratch_shapes=list(scratch),
        compiler_params=pltpu.CompilerParams(vmem_limit_bytes=16 << 20),
        cost_estimate=pl.CostEstimate(flops=flops, bytes_accessed=1 << 20, transcendentals=0),
    )


def edge_kernel(slots, rows, states_ref, diff_ref, vel_ref, last_ref, first_ref):
    for out_ref, base in ((last_ref, rows - STEPS), (first_ref, 0)):
        for j in range(STEPS):
            row = base + j
            out_ref[j, :slots, :] = states_ref[pl.ds(row, slots, stride=rows), :].astype(BF16)
            fields = []
            for field in (diff_ref[row : row + 1], vel_ref[0, row : row + 1], vel_ref[1, row : row + 1]):
                fields.extend(pieces(field))
            out_ref[j, slots:, :] = stacked(fields, PAD)


def forecast_kernel(
    slots, rows, counts_ref, rank_ref, states_ref, low_ref, high_ref, diff_ref, vel_ref, pick_ref,
    cells_ref, seen_ref, coef_ref, value_ref,
):
    columns = states_ref.shape[1]
    total_rows = rows + 2 * STEPS
    count = counts_ref[rank_ref[0]]

    for row in range(1, total_rows - 1):
        if STEPS <= row < STEPS + rows:
            own = row - STEPS
            diff, along, across = (
                diff_ref[own : own + 1], vel_ref[0, own : own + 1], vel_ref[1, own : own + 1],
            )
        else:
            block = (low_ref[row] if row < STEPS else high_ref[row - STEPS - rows])[slots:]
            diff, along, across = joined(block, 0), joined(block, 3), joined(block, 6)
        for index, coef in enumerate(
            (
                1.0 - 4.0 * diff,
                diff - 0.5 * along,
                diff + 0.5 * along,
                diff - 0.5 * across,
                diff + 0.5 * across,
            )
        ):
            coef_ref[row, index] = jnp.broadcast_to(coef, (8, columns))

    chunk = 16
    halves = chunk // 8
    sums = [jnp.zeros((8, columns), F32)] * rows
    for start in range(0, slots, chunk):
        values = []
        for row in range(total_rows):
            if row < STEPS:
                block = low_ref[row, start : start + chunk, :].astype(F32)
            elif row < STEPS + rows:
                block = states_ref[pl.ds(start * rows + row - STEPS, chunk, stride=rows), :]
            else:
                block = high_ref[row - STEPS - rows, start : start + chunk, :].astype(F32)
            values.append([block[8 * h : 8 * h + 8] for h in range(halves)])
        for step in range(STEPS):
            after = list(values)
            for row in range(step + 1, total_rows - step - 1):
                coefs = [coef_ref[row, index] for index in range(5)]
                new = []
                for h in range(halves):
                    u = values[row][h]
                    right = pltpu.roll(u, columns - 1, 1)
                    left = pltpu.roll(u, 1, 1)
                    new.append(
                        u * (coefs[0] - 0.05 * (u * u))
                        + coefs[1] * values[row + 1][h]
                        + coefs[2] * values[row - 1][h]
                        + coefs[3] * right
                        + coefs[4] * left
                    )
                after[row] = new
            values = after
        for h in range(halves):
            place = lax.broadcasted_iota(jnp.int32, (8, columns), 0) + (start + 8 * h)
            live = place < count
            for row in range(rows):
                u = jnp.where(live, values[row + STEPS][h], 0.0)
                sums[row] = sums[row] + u
                value_ref[row, start + 8 * h : start + 8 * h + 8, :] = u

    live = lax.broadcasted_iota(jnp.int32, (slots, columns), 0) < count
    inverse = 1.0 / jnp.full((1, columns), count, jnp.int32).astype(F32)
    for row in range(rows):
        mean = jnp.sum(sums[row], axis=0, keepdims=True) * inverse
        part = jnp.where(live, value_ref[row] - mean, 0.0).astype(BF16)
        cells_ref[:slots, row * columns : (row + 1) * columns] = part
        cells_ref[slots:, row * columns : (row + 1) * columns] = stacked(pieces(mean), PAD)
    seen_ref[...] = jnp.dot(
        cells_ref[...], pick_ref[...], preferred_element_type=F32
    ).astype(BF16)


def anomalies(slots, runners, members, counts_ref, rank_ref, block_refs):
    rank = rank_ref[0]
    mean = 0.0
    own_means = []
    for step, block_ref in enumerate(block_refs):
        count = counts_ref[source_of(runners, step, rank)]
        row = joined(block_ref[slots:, :], 0)
        own_means.append(row)
        mean = mean + row * jnp.full(row.shape, count, jnp.int32).astype(F32)
    mean = mean * (1.0 / members)
    parts = []
    for step, block_ref in enumerate(block_refs):
        count = counts_ref[source_of(runners, step, rank)]
        live = lax.broadcasted_iota(jnp.int32, (slots, mean.shape[1]), 0) < count
        part = block_ref[:slots, :].astype(F32) + (own_means[step] - mean)
        parts.append(jnp.where(live, part, 0.0).astype(BF16))
    return parts, mean


def placing(slots, runners, members, counts_ref, runner, by_slot):
    shape, slot_dim = ((slots, members), 0) if by_slot else ((members, slots), 1)
    slot = lax.broadcasted_iota(jnp.int32, shape, slot_dim)
    member = lax.broadcasted_iota(jnp.int32, shape, 1 - slot_dim)
    offset = offset_of(counts_ref, runner, runners)
    hit = (member - slot == offset) & (slot < counts_ref[runner])
    return jnp.where(hit, 1.0, 0.0).astype(BF16)


def gram_kernel(slots, runners, members, counts_ref, rank_ref, *refs):
    seen_refs, (value_ref, weight_ref, out_ref) = refs[:runners], refs[runners:]
    rank = rank_ref[0]
    parts, mean = anomalies(slots, runners, members, counts_ref, rank_ref, seen_refs)
    observed = 0.0
    for step, part in enumerate(parts):
        place = placing(
            slots, runners, members, counts_ref, source_of(runners, step, rank), False
        )
        observed = observed + jnp.dot(place, part, preferred_element_type=F32)
    weighted = (observed * weight_ref[...]).astype(BF16)
    across = (((1,), (1,)), ((), ()))
    gram = lax.dot_general(
        weighted, observed.astype(BF16), across, preferred_element_type=F32
    )
    innovation = stacked(pieces(value_ref[...] - mean), PAD)
    bias = lax.dot_general(innovation, weighted, across, preferred_element_type=F32)
    out_ref[:members, :] = gram.astype(BF16)
    out_ref[members:, :] = stacked(pieces(bias[0:1] + bias[1:2] + bias[2:3]), PAD)


def sum_kernel(members, *refs):
    part_refs, out_ref = refs[:-1], refs[-1]
    gram, bias = total_of(members, part_refs)
    out_ref[:members, :] = gram.astype(BF16)
    out_ref[members:, :] = stacked(pieces(bias), PAD)


def total_of(members, part_refs):
    gram, bias = 0.0, 0.0
    for ref in part_refs:
        gram = gram + ref[:members, :].astype(F32)
        bias = bias + joined(ref[members:, :], 0)
    return gram, bias


def cells_kernel(slots, runners, members, counts_ref, rank_ref, *refs):
    cells_refs, (out_ref, mean_ref) = refs[:runners], refs[runners:]
    parts, mean = anomalies(slots, runners, members, counts_ref, rank_ref, cells_refs)
    for step, part in enumerate(parts):
        out_ref[step * slots : (step + 1) * slots, :] = part
    mean_ref[...] = jnp.broadcast_to(mean, mean_ref.shape)


def final_kernel(slots, rows, runners, members, counts_ref, rank_ref, *refs):
    part_refs, (cells_ref, mean_ref, out_ref) = refs[:-3], refs[-3:]
    rank = rank_ref[0]
    gram, bias = total_of(members, part_refs)
    row_id = lax.broadcasted_iota(jnp.int32, (members, members), 0)
    column_id = lax.broadcasted_iota(jnp.int32, (members, members), 1)
    diagonal = row_id == column_id
    trace = jnp.sum(
        jnp.sum(jnp.where(diagonal, gram, 0.0), axis=0, keepdims=True), axis=1, keepdims=True
    )
    scaling = float(members) / trace
    scaled = (gram * scaling).astype(BF16)
    square = jnp.dot(scaled, scaled, preferred_element_type=F32).astype(BF16)
    cubed = jnp.dot(square, scaled, preferred_element_type=F32)
    transform = (
        jnp.where(diagonal, 1.0, 0.0)
        - 0.5 * scaled.astype(F32)
        + 0.375 * square.astype(F32)
        - 0.3125 * cubed
    )
    bias = jnp.broadcast_to((bias * scaling).astype(BF16).astype(F32), (8, members))
    shift = lax.dot_general(
        bias, transform, (((1,), (1,)), ((), ())),
        preferred_element_type=F32, precision=lax.Precision.HIGHEST,
    )[0:1]
    own = placing(slots, runners, members, counts_ref, rank, True)
    own_rows = jnp.dot(own, transform.astype(BF16), preferred_element_type=F32).astype(BF16)
    spread = stacked(pieces(shift), PAD)
    result = 0.0
    for step in range(runners):
        place = placing(
            slots, runners, members, counts_ref, source_of(runners, step, rank), False
        )
        part = cells_ref[step * slots : (step + 1) * slots, :]
        left = jnp.concatenate(
            [
                jnp.dot(own_rows, place, preferred_element_type=F32).astype(BF16),
                jnp.dot(spread, place, preferred_element_type=F32).astype(BF16),
            ],
            axis=0,
        )
        result = result + jnp.dot(left, part, preferred_element_type=F32)
    columns = out_ref.shape[1]
    live = lax.broadcasted_iota(jnp.int32, (slots, columns), 0) < counts_ref[rank]
    shifted = (
        mean_ref[0:1, :]
        + result[slots : slots + 1]
        + result[slots + 1 : slots + 2]
        + result[slots + 2 : slots + 3]
    )
    for row in range(rows):
        span = slice(row * columns, (row + 1) * columns)
        out_ref[pl.ds(row, slots, stride=rows), :] = jnp.where(
            live, result[:slots, span] + shifted[:, span], 0.0
        )


def body(states, diffusivity, velocity, counts, obs_index, obs_value, obs_weight):
    runners = lax.axis_size("runner")
    blocks = lax.axis_size("cells")
    slots, rows, columns = states.shape
    members = slots // 2 * runners
    cells = rows * columns
    seen = obs_index.shape[0]
    height = slots + PAD
    shape = jax.ShapeDtypeStruct

    rank = lax.axis_index("runner").astype(jnp.int32).reshape(1)
    flat = states.reshape(slots * rows, columns)
    last, first = call(
        functools.partial(edge_kernel, slots, rows),
        [shape((STEPS, height, columns), BF16)] * 2,
        3,
    )(flat, diffusivity, velocity)
    forward = [(i, (i + 1) % blocks) for i in range(blocks)]
    backward = [(target, source) for source, target in forward]
    low = lax.ppermute(last, "cells", forward)
    high = lax.ppermute(first, "cells", backward)
    pick = (
        lax.broadcasted_iota(jnp.int32, (cells, seen), 0) == obs_index[None, :]
    ).astype(BF16)

    own_cells, own_seen = call(
        functools.partial(forecast_kernel, slots, rows),
        [shape((height, cells), BF16), shape((height, seen), BF16)],
        6,
        2,
        scratch=[
            pltpu.VMEM((rows + 2 * STEPS, 5, 8, columns), F32),
            pltpu.VMEM((rows, slots, columns), F32),
        ],
    )(counts, rank, flat, low, high, diffusivity, velocity, pick)

    all_seen = [own_seen] + [
        lax.ppermute(own_seen, "runner", partners(runners, step)) for step in range(1, runners)
    ]
    all_cells = [own_cells] + [
        lax.ppermute(own_cells, "runner", partners(runners, step)) for step in range(1, runners)
    ]

    part = call(
        functools.partial(gram_kernel, slots, runners, members),
        shape((members + PAD, members), BF16),
        runners + 2,
        2,
    )(counts, rank, *all_seen, obs_value[None, :], obs_weight[None, :])

    stages = [[1]]
    width = 2
    while width < blocks:
        reach = min(4, blocks // width)
        stages.append([width * step for step in range(1, reach)])
        width = width * reach
    for index, stage in enumerate(stages):
        parts = [part] + [lax.ppermute(part, "cells", partners(blocks, step)) for step in stage]
        if index + 1 < len(stages):
            part = call(
                functools.partial(sum_kernel, members),
                shape((members + PAD, members), BF16),
                len(parts),
            )(*parts)

    anomaly, mean = call(
        functools.partial(cells_kernel, slots, runners, members),
        [shape((runners * slots, cells), BF16), shape((8, cells), F32)],
        runners,
        2,
    )(counts, rank, *all_cells)
    result = call(
        functools.partial(final_kernel, slots, rows, runners, members),
        shape((slots * rows, columns), F32),
        len(parts) + 2,
        2,
    )(counts, rank, *parts, anomaly, mean)
    return result.reshape(slots, rows, columns)


def solution(mesh):
    return jax.shard_map(
        body,
        mesh=mesh,
        in_specs=(
            P("runner", "cells", None),
            P("cells", None),
            P(None, "cells", None),
            P(),
            P("cells"),
            P("cells"),
            P("cells"),
        ),
        out_specs=P("runner", "cells", None),
        check_vma=False,
    )
```

```python
import functools

import jax
import jax.numpy as jnp
from jax import lax
from jax.experimental import pallas as pl
from jax.experimental.pallas import tpu as pltpu
from jax.sharding import PartitionSpec as P


STEPS = 4
PAD = 16
F32 = jnp.float32
BF16 = jnp.bfloat16

PARTS = 2


def partners(count, step):
    return [(i, i ^ step) for i in range(count)]


def pieces(row):
    high = row.astype(BF16).astype(F32)
    rest = row - high
    middle = rest.astype(BF16).astype(F32)
    return high, middle, rest - middle


def stacked(rows, height, dtype=BF16):
    width = rows[0].shape[1]
    place = lax.broadcasted_iota(jnp.int32, (height, width), 0)
    total = jnp.zeros((height, width), F32)
    for index, row in enumerate(rows):
        total = jnp.where(place == index, row, total)
    return total.astype(dtype)


def joined(block, first):
    block = block.astype(F32)
    return block[first : first + 1] + block[first + 1 : first + 2] + block[first + 2 : first + 3]


def offset_of(counts_ref, runner, runners):
    total = jnp.int32(0)
    for index in range(runners):
        total = total + jnp.where(index < runner, counts_ref[index], 0)
    return total


def as_row(scalar, width):
    return jnp.full((1, width), scalar, jnp.int32).astype(F32)


def size_of(shape):
    size = shape.dtype.itemsize
    for extent in shape.shape:
        size = size * extent
    return size


def call(kernel, out_shape, scalars, vectors, scratch=()):
    vector = pl.BlockSpec(memory_space=pltpu.VMEM)
    scalar = pl.BlockSpec(memory_space=pltpu.SMEM)
    many = isinstance(out_shape, list)
    shapes = list(vectors) + (out_shape if many else [out_shape])
    held = sum(size_of(shape) for shape in shapes)
    return pl.pallas_call(
        kernel,
        out_shape=out_shape,
        in_specs=[scalar] * len(scalars) + [vector] * len(vectors),
        out_specs=[vector] * len(out_shape) if many else vector,
        scratch_shapes=list(scratch),
        compiler_params=pltpu.CompilerParams(
            vmem_limit_bytes=min(56 << 20, (12 << 20) + 3 * held)
        ),
        cost_estimate=pl.CostEstimate(flops=0, bytes_accessed=1 << 20, transcendentals=0),
    )(*scalars, *vectors)


def edge_kernel(slots, rows, states_ref, fields_ref, last_ref, first_ref):
    for out_ref, base in ((last_ref, rows - STEPS), (first_ref, 0)):
        for j in range(STEPS):
            row = base + j
            out_ref[j, :slots, :] = states_ref[pl.ds(row, slots, stride=rows), :].astype(BF16)
            packed = []
            for field in range(3):
                packed.extend(pieces(fields_ref[field, row : row + 1]))
            out_ref[j, slots:, :] = stacked(packed, PAD)


def forecast_kernel(
    slots, rows, shares, counts_ref, rank_ref, states_ref, low_ref, high_ref, fields_ref, pick_ref,
    *rest,
):
    (coef_ref, value_ref, cells_ref) = rest[-3:]
    seen_refs, part_refs = rest[:shares], rest[shares:-3]
    columns = states_ref.shape[1]
    total_rows = rows + 2 * STEPS
    count = counts_ref[rank_ref[0]]

    for row in range(1, total_rows - 1):
        if STEPS <= row < STEPS + rows:
            own = row - STEPS
            diff, along, across = (fields_ref[field, own : own + 1] for field in range(3))
        else:
            block = (low_ref[row] if row < STEPS else high_ref[row - STEPS - rows])[slots:]
            diff, along, across = joined(block, 0), joined(block, 3), joined(block, 6)
        for index, coef in enumerate(
            (
                1.0 - 4.0 * diff,
                diff - 0.5 * along,
                diff + 0.5 * along,
                diff - 0.5 * across,
                diff + 0.5 * across,
            )
        ):
            coef_ref[row, index] = jnp.broadcast_to(coef, (8, columns))

    chunk = 16
    halves = chunk // 8
    sums = [jnp.zeros((8, columns), F32)] * rows
    for start in range(0, slots, chunk):
        values = []
        for row in range(total_rows):
            if row < STEPS:
                block = low_ref[row, start : start + chunk, :].astype(F32)
            elif row < STEPS + rows:
                block = states_ref[pl.ds(start * rows + row - STEPS, chunk, stride=rows), :]
            else:
                block = high_ref[row - STEPS - rows, start : start + chunk, :].astype(F32)
            values.append([block[8 * h : 8 * h + 8] for h in range(halves)])
        for step in range(STEPS):
            after = list(values)
            for row in range(step + 1, total_rows - step - 1):
                coefs = [coef_ref[row, index] for index in range(5)]
                new = []
                for h in range(halves):
                    u = values[row][h]
                    right = pltpu.roll(u, columns - 1, 1)
                    left = pltpu.roll(u, 1, 1)
                    new.append(
                        u * (coefs[0] - 0.05 * (u * u))
                        + coefs[1] * values[row + 1][h]
                        + coefs[2] * values[row - 1][h]
                        + coefs[3] * right
                        + coefs[4] * left
                    )
                after[row] = new
            values = after
        for h in range(halves):
            place = lax.broadcasted_iota(jnp.int32, (8, columns), 0) + (start + 8 * h)
            live = place < count
            for row in range(rows):
                u = jnp.where(live, values[row + STEPS][h], 0.0)
                sums[row] = sums[row] + u
                value_ref[row, start + 8 * h : start + 8 * h + 8, :] = u

    live = lax.broadcasted_iota(jnp.int32, (slots, columns), 0) < count
    inverse = 1.0 / as_row(count, columns)
    means = []
    for row in range(rows):
        mean = jnp.sum(sums[row], axis=0, keepdims=True) * inverse
        part = jnp.where(live, value_ref[row] - mean, 0.0).astype(BF16)
        cells_ref[:slots, row * columns : (row + 1) * columns] = part
        cells_ref[slots:, row * columns : (row + 1) * columns] = stacked(pieces(mean), PAD)
        means.append(mean)
    width = rows * columns // len(part_refs)
    for index, part_ref in enumerate(part_refs):
        part_ref[...] = cells_ref[:slots, index * width : (index + 1) * width]
    seen = jnp.dot(cells_ref[...], pick_ref[...], preferred_element_type=F32)
    share = seen.shape[1] // shares
    packed = [jnp.zeros((1, share), F32)] * 3
    for first in range(0, rows, share // columns):
        packed.extend(
            pieces(jnp.concatenate(means[first : first + share // columns], axis=1))
        )
    packed = stacked(packed, seen_refs[0].shape[0] - slots)
    for index, seen_ref in enumerate(seen_refs):
        part = seen[:, index * share : (index + 1) * share].astype(BF16)
        seen_ref[:slots, :] = part[:slots]
        seen_ref[slots : slots + PAD, :] = part[slots:] + packed[:PAD]
        if packed.shape[0] > PAD:
            seen_ref[slots + PAD :, :] = packed[PAD:]


def placing(slots, runners, members, counts_ref, runner, by_slot):
    shape, slot_dim = ((slots, members), 0) if by_slot else ((members, slots), 1)
    slot = lax.broadcasted_iota(jnp.int32, shape, slot_dim)
    member = lax.broadcasted_iota(jnp.int32, shape, 1 - slot_dim)
    offset = offset_of(counts_ref, runner, runners)
    hit = (member - slot == offset) & (slot < counts_ref[runner])
    return jnp.where(hit, 1.0, 0.0).astype(BF16)


def triangles(members):
    half = members // 2
    row = lax.broadcasted_iota(jnp.int32, (half, half), 0)
    column = lax.broadcasted_iota(jnp.int32, (half, half), 1)
    return half, row, column


def gram_kernel(slots, runners, members, counts_ref, rank_ref, *refs):
    seen_refs, (value_ref, weight_ref, out_ref) = refs[:runners], refs[runners:]
    rank = rank_ref[0]
    counts = [counts_ref[rank ^ step] for step in range(runners)]
    own_means = [joined(ref[slots:, :], 0) for ref in seen_refs]
    width = value_ref.shape[1]
    mean = 0.0
    for row, count in zip(own_means, counts):
        mean = mean + row * as_row(count, width)
    mean = mean * (1.0 / members)
    observed = 0.0
    for step, ref in enumerate(seen_refs):
        live = lax.broadcasted_iota(jnp.int32, (slots, width), 0) < counts[step]
        part = ref[:slots, :].astype(F32) + (own_means[step] - mean)
        part = jnp.where(live, part, 0.0).astype(BF16)
        place = placing(slots, runners, members, counts_ref, rank ^ step, False)
        observed = observed + jnp.dot(place, part, preferred_element_type=F32)
    weighted = (observed * weight_ref[...]).astype(BF16)
    across = (((1,), (1,)), ((), ()))
    gram = lax.dot_general(
        weighted, observed.astype(BF16), across, preferred_element_type=F32
    )
    innovation = stacked(pieces(value_ref[...] - mean), PAD)
    bias = lax.dot_general(innovation, weighted, across, preferred_element_type=F32)
    half, row, column = triangles(members)
    last = gram[half:, half:]
    out_ref[:half, :half] = jnp.where(row >= column, gram[:half, :half], last)
    out_ref[:half, half:] = gram[:half, half:]
    diagonal = jnp.sum(jnp.where(row == column, last, 0.0), axis=0, keepdims=True)
    diagonal = jnp.concatenate([diagonal, jnp.zeros_like(diagonal)], axis=1)
    out_ref[half:, :] = stacked([bias[0:1] + bias[1:2] + bias[2:3], diagonal], 8, F32)


def total_of(half, part_refs):
    packed, bias, diagonal = 0.0, 0.0, 0.0
    for ref in part_refs:
        packed = packed + ref[:half, :].astype(F32)
        if ref.dtype == BF16:
            bias = bias + joined(ref[half:, :], 0)
            diagonal = diagonal + joined(ref[half:, :], 3)
        else:
            bias = bias + ref[half : half + 1, :]
            diagonal = diagonal + ref[half + 1 : half + 2, :]
    return packed, bias, diagonal


def sum_kernel(half, *refs):
    part_refs, out_ref = refs[:-1], refs[-1]
    packed, bias, diagonal = total_of(half, part_refs)
    out_ref[:half, :] = packed.astype(BF16)
    out_ref[half:, :] = stacked([*pieces(bias), *pieces(diagonal)], PAD)


def transform_kernel(slots, runners, members, counts_ref, rank_ref, *refs):
    part_refs, out_refs = refs[:-2], refs[-2:]
    rank = rank_ref[0]
    half, row, column = triangles(members)
    packed, bias, diagonal = total_of(half, part_refs)
    corner, side = packed[:, :half], packed[:, half:]
    mirror = jnp.transpose(corner)
    first = jnp.where(row >= column, corner, mirror)
    last = jnp.where(
        row < column, corner, jnp.where(row == column, diagonal[:, :half], mirror)
    )
    gram = jnp.concatenate(
        [
            jnp.concatenate([first, side], axis=1),
            jnp.concatenate([jnp.transpose(side), last], axis=1),
        ],
        axis=0,
    )
    trace = jnp.sum(
        jnp.sum(jnp.where(row == column, first + last, 0.0), axis=0, keepdims=True),
        axis=1, keepdims=True,
    )
    scaling = float(members) / trace
    scaled = (gram * scaling).astype(BF16)
    bias = (bias * scaling).astype(BF16).astype(F32)

    def times(left):
        return jnp.dot(left, scaled, preferred_element_type=F32)

    first_power = times(jnp.concatenate([scaled, stacked([bias], PAD)], axis=0))
    square = first_power[:members].astype(BF16)
    bias_1 = first_power[members : members + 1]
    second_power = times(jnp.concatenate([square, stacked(pieces(bias_1), PAD)], axis=0))
    cubed = second_power[:members]
    bias_2 = joined(second_power[members:], 0)
    bias_3 = joined(times(stacked(pieces(bias_2), PAD)), 0)
    shift = bias - 0.5 * bias_1 + 0.375 * bias_2 - 0.3125 * bias_3
    identity = lax.broadcasted_iota(jnp.int32, (members, members), 0) == (
        lax.broadcasted_iota(jnp.int32, (members, members), 1)
    )
    transform = (
        jnp.where(identity, 1.0, 0.0)
        - 0.5 * scaled.astype(F32)
        + 0.375 * square.astype(F32)
        - 0.3125 * cubed
    ).astype(BF16)
    places = [
        placing(slots, runners, members, counts_ref, rank ^ step, False)
        for step in range(0, runners, 2)
    ]
    shift = stacked(pieces(shift), PAD)
    for side, out_ref in enumerate(out_refs):
        own = placing(slots, runners, members, counts_ref, rank ^ (1 - side), True)
        rows = jnp.dot(own, transform, preferred_element_type=F32).astype(BF16)
        left = jnp.concatenate([rows, shift], axis=0)
        for index, place in enumerate(places):
            out_ref[:, index * slots : (index + 1) * slots] = jnp.dot(
                left, place, preferred_element_type=F32
            ).astype(BF16)


def own_means_of(slots, members, counts_ref, rank, seen_refs, cells):
    share = seen_refs[0].shape[1]
    own_means, mean = [], 0.0
    for step, ref in enumerate(seen_refs):
        packed = ref[slots:, :]
        row = jnp.concatenate(
            [joined(packed, 3 + 3 * index) for index in range(cells // share)], axis=1
        )
        own_means.append(row)
        mean = mean + row * as_row(counts_ref[rank ^ step], cells)
    return own_means, mean * (1.0 / members)


def product_kernel(slots, members, runners, with_mean, counts_ref, rank_ref, left_ref, *refs):
    parts = len(refs) - runners
    parts = parts // (runners // 2 + 1)
    seen_refs, cell_refs, out_refs = refs[:runners], refs[runners:-parts], refs[-parts:]
    width = out_refs[0].shape[1]
    own_means, mean = own_means_of(
        slots, members, counts_ref, rank_ref[0], seen_refs, width * parts
    )
    lefts = [
        left_ref[:, index * slots : (index + 1) * slots] for index in range(runners // 2)
    ]
    sums = [jnp.sum(left.astype(F32), axis=1, keepdims=True) for left in lefts]
    for part, out_ref in enumerate(out_refs):
        span = slice(part * width, (part + 1) * width)
        total = 0.0
        for index, left in enumerate(lefts):
            total = total + jnp.dot(
                left, cell_refs[index * parts + part][...], preferred_element_type=F32
            )
            total = total + sums[index] * (own_means[2 * index] - mean)[:, span]
        shift = joined(total[slots:], 0)
        if with_mean:
            shift = shift + mean[:, span]
        out_ref[...] = (total[:slots] + shift).astype(out_ref.dtype)


def final_kernel(slots, rows, counts_ref, rank_ref, *refs):
    own_refs, other_refs, out_ref = refs[: len(refs) // 2], refs[len(refs) // 2 : -1], refs[-1]
    columns = out_ref.shape[1]
    live = lax.broadcasted_iota(jnp.int32, (slots, columns), 0) < counts_ref[rank_ref[0]]
    row = 0
    for own_ref, other_ref in zip(own_refs, other_refs):
        for first in range(0, own_ref.shape[1], columns):
            span = slice(first, first + columns)
            out_ref[pl.ds(row, slots, stride=rows), :] = jnp.where(
                live, own_ref[:, span] + other_ref[:, span].astype(F32), 0.0
            )
            row = row + 1


def body(states, diffusivity, velocity, counts, obs_index, obs_value, obs_weight):
    runners = lax.axis_size("runner")
    blocks = lax.axis_size("cells")
    slots, rows, columns = states.shape
    members = slots // 2 * runners
    half = members // 2
    cells = rows * columns
    seen = obs_index.shape[0]
    shares = 2
    share = seen // shares
    height = slots + PAD
    shape = jax.ShapeDtypeStruct

    rank = lax.axis_index("runner").astype(jnp.int32).reshape(1)
    parity = rank[0] % shares
    flat = states.reshape(slots * rows, columns)
    fields = jnp.concatenate([diffusivity[None], velocity], axis=0)
    last, first = call(
        functools.partial(edge_kernel, slots, rows),
        [shape((STEPS, height, columns), BF16)] * 2,
        [],
        [flat, fields],
    )
    forward = [(i, (i + 1) % blocks) for i in range(blocks)]
    backward = [(target, source) for source, target in forward]
    low = lax.ppermute(last, "cells", forward)
    high = lax.ppermute(first, "cells", backward)

    def own_first(array):
        return jnp.where(parity == 0, array, jnp.roll(array, -share))

    pick = (
        lax.broadcasted_iota(jnp.int32, (cells, seen), 0) == own_first(obs_index)[None, :]
    ).astype(BF16)
    own_value = own_first(obs_value)[None, :share]
    own_weight = own_first(obs_weight)[None, :share]

    lower = -(-(3 + 3 * (cells // share)) // PAD) * PAD
    kept, given, *own_cells = call(
        functools.partial(forecast_kernel, slots, rows, shares),
        [shape((slots + lower, share), BF16)] * shares
        + [shape((slots, cells // PARTS), BF16)] * PARTS,
        [counts, rank],
        [flat, low, high, fields, pick],
        [
            pltpu.VMEM((rows + 2 * STEPS, 5, 8, columns), F32),
            pltpu.VMEM((rows, slots, columns), F32),
            pltpu.VMEM((height, cells), BF16),
        ],
    )

    def moved(array, bit, axis="runner"):
        return lax.ppermute(array, axis, partners(lax.axis_size(axis), bit))

    all_seen = [kept] + [
        moved(given if step % shares else kept, step)
        for step in range(1, runners)
    ]
    all_cells = {0: own_cells}
    bit = runners // 2
    while bit > 1:
        for step in list(all_cells):
            all_cells[step + bit] = [moved(array, bit) for array in all_cells[step]]
        bit = bit // 2
    held = [array for step in sorted(all_cells) for array in all_cells[step]]

    part = call(
        functools.partial(gram_kernel, slots, runners, members),
        shape((half + 8, members), F32),
        [counts, rank],
        [*all_seen, own_value, own_weight],
    )
    stages = [("cells", [1]), ("runner", [1])]
    width = 2
    while width < blocks:
        reach = min(4, blocks // width)
        stages.append(("cells", [width * step for step in range(1, reach)]))
        width = width * reach
    for index, (axis, stage) in enumerate(stages):
        parts = [part] + [moved(part, step, axis) for step in stage]
        if index + 1 < len(stages):
            part = call(
                functools.partial(sum_kernel, half),
                shape((half + PAD, members), BF16),
                [],
                parts,
            )
    give, keep = call(
        functools.partial(transform_kernel, slots, runners, members),
        [shape((height, runners // 2 * slots), BF16)] * 2,
        [counts, rank],
        parts,
    )
    given_products = call(
        functools.partial(product_kernel, slots, members, runners, False),
        [shape((slots, cells // PARTS), BF16)] * PARTS,
        [counts, rank],
        [give, *all_seen, *held],
    )
    other_products = [moved(array, 1) for array in given_products]
    own_products = call(
        functools.partial(product_kernel, slots, members, runners, True),
        [shape((slots, cells // PARTS), F32)] * PARTS,
        [counts, rank],
        [keep, *all_seen, *held],
    )
    analysed = call(
        functools.partial(final_kernel, slots, rows),
        shape((slots * rows, columns), F32),
        [counts, rank],
        [*own_products, *other_products],
    )
    return analysed.reshape(slots, rows, columns)


def solution(mesh):
    return jax.shard_map(
        body,
        mesh=mesh,
        in_specs=(
            P("runner", "cells", None),
            P("cells", None),
            P(None, "cells", None),
            P(),
            P("cells"),
            P("cells"),
            P("cells"),
        ),
        out_specs=P("runner", "cells", None),
        check_vma=False,
    )
```

```python
import functools

import jax
import jax.numpy as jnp
from jax import lax
from jax.experimental import pallas as pl
from jax.experimental.pallas import tpu as pltpu
from jax.sharding import PartitionSpec as P


STEPS = 4
PAD = 16
F32 = jnp.float32
BF16 = jnp.bfloat16

PARTS = 2
WRITES = 4
GATHERED = 1


def partners(count, step):
    return [(i, i ^ step) for i in range(count)]


def pieces(row):
    high = row.astype(BF16).astype(F32)
    rest = row - high
    middle = rest.astype(BF16).astype(F32)
    return high, middle, rest - middle


def stacked(rows, height, dtype=BF16):
    width = rows[0].shape[1]
    place = lax.broadcasted_iota(jnp.int32, (height, width), 0)
    total = jnp.zeros((height, width), F32)
    for index, row in enumerate(rows):
        total = jnp.where(place == index, row, total)
    return total.astype(dtype)


def joined(block, first):
    block = block.astype(F32)
    return block[first : first + 1] + block[first + 1 : first + 2] + block[first + 2 : first + 3]


def offset_of(counts_ref, runner, runners):
    total = jnp.int32(0)
    for index in range(runners):
        total = total + jnp.where(index < runner, counts_ref[index], 0)
    return total


def as_row(scalar, width):
    return jnp.full((1, width), scalar, jnp.int32).astype(F32)


def size_of(shape):
    size = shape.dtype.itemsize
    for extent in shape.shape:
        size = size * extent
    return size


def call(kernel, out_shape, scalars, vectors, scratch=(), outside=False, write=False):
    vector = pl.BlockSpec(memory_space=pltpu.VMEM)
    scalar = pl.BlockSpec(memory_space=pltpu.SMEM)
    hbm = pl.BlockSpec(memory_space=pltpu.HBM)
    if outside:
        vectors = [pltpu.with_memory_space_constraint(array, pltpu.HBM) for array in vectors]
    many = isinstance(out_shape, list)
    shapes = list(vectors) + (out_shape if many else [out_shape])
    held = sum(size_of(shape) for shape in shapes)
    return pl.pallas_call(
        kernel,
        out_shape=out_shape,
        in_specs=[scalar] * len(scalars) + [hbm if outside else vector] * len(vectors),
        out_specs=hbm if write else [vector] * len(out_shape) if many else vector,
        scratch_shapes=list(scratch),
        compiler_params=pltpu.CompilerParams(
            vmem_limit_bytes=min(56 << 20, (12 << 20) + 3 * held)
        ),
        cost_estimate=pl.CostEstimate(flops=0, bytes_accessed=1 << 20, transcendentals=0),
    )(*scalars, *vectors)


def edge_kernel(
    slots, rows, states_hbm, diff_hbm, vel_hbm, last_ref, first_ref, states_ref, fields_ref, sems
):
    copies = [
        pltpu.make_async_copy(states_hbm, states_ref, sems.at[0]),
        pltpu.make_async_copy(diff_hbm, fields_ref.at[0], sems.at[1]),
        pltpu.make_async_copy(vel_hbm, fields_ref.at[pl.ds(1, 2)], sems.at[2]),
    ]
    for copy in copies:
        copy.start()
    for copy in copies:
        copy.wait()
    for out_ref, base in ((last_ref, rows - STEPS), (first_ref, 0)):
        for j in range(STEPS):
            row = base + j
            out_ref[j, :slots, :] = states_ref[pl.ds(row, slots, stride=rows), :].astype(BF16)
            packed = []
            for field in range(3):
                packed.extend(pieces(fields_ref[field, row : row + 1]))
            out_ref[j, slots:, :] = stacked(packed, PAD)


def coefficients(diff, along, across):
    columns = diff.shape[1]
    return [
        jnp.broadcast_to(coef, (8, columns))
        for coef in (
            1.0 - 4.0 * diff,
            diff - 0.5 * along,
            diff + 0.5 * along,
            diff - 0.5 * across,
            diff + 0.5 * across,
        )
    ]


def advanced(u, above, below, coefs):
    columns = u.shape[1]
    return (
        u * (coefs[0] - 0.05 * (u * u))
        + coefs[1] * above
        + coefs[2] * below
        + coefs[3] * pltpu.roll(u, columns - 1, 1)
        + coefs[4] * pltpu.roll(u, 1, 1)
    )


def inner_rows(rows):
    return [range(step, rows - step) for step in range(1, STEPS) if step < rows - step]


def inner_kernel(slots, rows, states_ref, fields_ref, coef_ref, inner_ref):
    for row in range(rows):
        fields = [fields_ref[field, row : row + 1] for field in range(3)]
        for index, coef in enumerate(coefficients(*fields)):
            coef_ref[row, index] = coef
    for start in range(0, slots, 16):
        values = []
        for row in range(rows):
            block = states_ref[pl.ds(start * rows + row, 16, stride=rows), :]
            values.append([block[8 * h : 8 * h + 8] for h in range(2)])
        place = 0
        for inside in inner_rows(rows):
            after = list(values)
            for row in inside:
                coefs = [coef_ref[row, index] for index in range(5)]
                after[row] = [
                    advanced(values[row][h], values[row + 1][h], values[row - 1][h], coefs)
                    for h in range(2)
                ]
                for h in range(2):
                    inner_ref[place, start + 8 * h : start + 8 * h + 8, :] = after[row][h]
                place = place + 1
            values = after


def forecast_kernel(
    slots, rows, shares, counts_ref, rank_ref, states_ref, low_ref, high_ref, own_coef_ref,
    inner_ref, pick_ref, *rest,
):
    (coef_ref, value_ref, cells_ref) = rest[-3:]
    seen_refs, part_refs = rest[:shares], rest[shares:-3]
    columns = states_ref.shape[1]
    total_rows = rows + 2 * STEPS
    count = counts_ref[rank_ref[0]]

    for row in [*range(1, STEPS), *range(STEPS + rows, total_rows - 1)]:
        block = (low_ref[row] if row < STEPS else high_ref[row - STEPS - rows])[slots:]
        fields = [joined(block, 3 * field) for field in range(3)]
        for index, coef in enumerate(coefficients(*fields)):
            coef_ref[row, index] = coef

    known = {}
    for step, inside in enumerate(inner_rows(rows)):
        for row in inside:
            known[step, row + STEPS] = len(known)
    chunk = 16
    halves = chunk // 8
    sums = [jnp.zeros((8, columns), F32)] * rows
    for start in range(0, slots, chunk):
        values = []
        for row in range(total_rows):
            if row < STEPS:
                block = low_ref[row, start : start + chunk, :].astype(F32)
            elif row < STEPS + rows:
                block = states_ref[pl.ds(start * rows + row - STEPS, chunk, stride=rows), :]
            else:
                block = high_ref[row - STEPS - rows, start : start + chunk, :].astype(F32)
            values.append([block[8 * h : 8 * h + 8] for h in range(halves)])
        for step in range(STEPS):
            after = list(values)
            for row in range(step + 1, total_rows - step - 1):
                if (step, row) in known:
                    block = inner_ref[known[step, row], start : start + chunk, :]
                    after[row] = [block[8 * h : 8 * h + 8] for h in range(halves)]
                    continue
                if STEPS <= row < STEPS + rows:
                    coefs = [own_coef_ref[row - STEPS, index] for index in range(5)]
                else:
                    coefs = [coef_ref[row, index] for index in range(5)]
                after[row] = [
                    advanced(values[row][h], values[row + 1][h], values[row - 1][h], coefs)
                    for h in range(halves)
                ]
            values = after
        for h in range(halves):
            place = lax.broadcasted_iota(jnp.int32, (8, columns), 0) + (start + 8 * h)
            live = place < count
            for row in range(rows):
                u = jnp.where(live, values[row + STEPS][h], 0.0)
                sums[row] = sums[row] + u
                value_ref[row, start + 8 * h : start + 8 * h + 8, :] = u

    live = lax.broadcasted_iota(jnp.int32, (slots, columns), 0) < count
    inverse = 1.0 / as_row(count, columns)
    means = []
    for row in range(rows):
        mean = jnp.sum(sums[row], axis=0, keepdims=True) * inverse
        part = jnp.where(live, value_ref[row] - mean, 0.0).astype(BF16)
        cells_ref[:slots, row * columns : (row + 1) * columns] = part
        cells_ref[slots:, row * columns : (row + 1) * columns] = stacked(pieces(mean), PAD)
        means.append(mean)
    width = rows * columns // len(part_refs)
    for index, part_ref in enumerate(part_refs):
        part_ref[...] = cells_ref[:slots, index * width : (index + 1) * width]
    seen = jnp.dot(cells_ref[...], pick_ref[...], preferred_element_type=F32)
    share = seen.shape[1] // shares
    packed = [jnp.zeros((1, share), F32)] * 3
    for first in range(0, rows, share // columns):
        packed.extend(
            pieces(jnp.concatenate(means[first : first + share // columns], axis=1))
        )
    packed = stacked(packed, seen_refs[0].shape[0] - slots)
    for index, seen_ref in enumerate(seen_refs):
        part = seen[:, index * share : (index + 1) * share].astype(BF16)
        seen_ref[:slots, :] = part[:slots]
        seen_ref[slots : slots + PAD, :] = part[slots:] + packed[:PAD]
        if packed.shape[0] > PAD:
            seen_ref[slots + PAD :, :] = packed[PAD:]


def placing(slots, runners, members, counts_ref, runner, by_slot):
    shape, slot_dim = ((slots, members), 0) if by_slot else ((members, slots), 1)
    slot = lax.broadcasted_iota(jnp.int32, shape, slot_dim)
    member = lax.broadcasted_iota(jnp.int32, shape, 1 - slot_dim)
    offset = offset_of(counts_ref, runner, runners)
    hit = (member - slot == offset) & (slot < counts_ref[runner])
    return jnp.where(hit, 1.0, 0.0).astype(BF16)


def setup_kernel(
    slots, runners, members, shares, counts_ref, rank_ref, index_ref, value_ref, weight_ref,
    pick_ref, seen_ref, place_ref, own_ref,
):
    rank = rank_ref[0]
    share = index_ref.shape[1] // shares

    def own_first(ref):
        swapped = jnp.concatenate([ref[:, share:], ref[:, :share]], axis=1)
        return jnp.where(jnp.bitwise_and(rank, 1) == 0, ref[...], swapped)

    wanted = own_first(index_ref)
    cell = lax.broadcasted_iota(jnp.int32, pick_ref.shape, 0)
    pick_ref[...] = jnp.where(cell == wanted, 1.0, 0.0).astype(BF16)
    seen_ref[...] = stacked([own_first(value_ref)[:, :share], own_first(weight_ref)[:, :share]], 8, F32)
    for step in range(runners):
        place_ref[:, step * slots : (step + 1) * slots] = placing(
            slots, runners, members, counts_ref, rank ^ step, False
        )
    for side in range(2):
        own_ref[side] = placing(slots, runners, members, counts_ref, rank ^ (1 - side), True)


def triangles(members):
    half = members // 2
    row = lax.broadcasted_iota(jnp.int32, (half, half), 0)
    column = lax.broadcasted_iota(jnp.int32, (half, half), 1)
    return half, row, column


def gram_kernel(slots, runners, members, counts_ref, rank_ref, *refs):
    seen_refs, (both_ref, place_ref, out_ref) = refs[:runners], refs[runners:]
    rank = rank_ref[0]
    counts = [counts_ref[rank ^ step] for step in range(runners)]
    own_means = [joined(ref[slots:, :], 0) for ref in seen_refs]
    width = both_ref.shape[1]
    mean = 0.0
    for row, count in zip(own_means, counts):
        mean = mean + row * as_row(count, width)
    mean = mean * (1.0 / members)
    observed = 0.0
    for step, ref in enumerate(seen_refs):
        live = lax.broadcasted_iota(jnp.int32, (slots, width), 0) < counts[step]
        part = ref[:slots, :].astype(F32) + (own_means[step] - mean)
        part = jnp.where(live, part, 0.0).astype(BF16)
        place = place_ref[:, step * slots : (step + 1) * slots]
        observed = observed + jnp.dot(place, part, preferred_element_type=F32)
    weighted = (observed * both_ref[1:2, :]).astype(BF16)
    across = (((1,), (1,)), ((), ()))
    gram = lax.dot_general(
        weighted, observed.astype(BF16), across, preferred_element_type=F32
    )
    innovation = stacked(pieces(both_ref[0:1, :] - mean), PAD)
    bias = lax.dot_general(innovation, weighted, across, preferred_element_type=F32)
    half, row, column = triangles(members)
    last = gram[half:, half:]
    out_ref[:half, :half] = jnp.where(row >= column, gram[:half, :half], last).astype(BF16)
    out_ref[:half, half:] = gram[:half, half:].astype(BF16)
    diagonal = jnp.sum(jnp.where(row == column, last, 0.0), axis=0, keepdims=True)
    diagonal = jnp.concatenate([diagonal, jnp.zeros_like(diagonal)], axis=1)
    out_ref[half:, :] = stacked([*pieces(joined(bias, 0)), *pieces(diagonal)], PAD)


def total_of(half, part_refs):
    packed, bias, diagonal = 0.0, 0.0, 0.0
    for ref in part_refs:
        packed = packed + ref[:half, :].astype(F32)
        bias = bias + joined(ref[half:, :], 0)
        diagonal = diagonal + joined(ref[half:, :], 3)
    return packed, bias, diagonal


def sum_kernel(half, *refs):
    part_refs, out_ref = refs[:-1], refs[-1]
    packed, bias, diagonal = total_of(half, part_refs)
    out_ref[:half, :] = packed.astype(BF16)
    out_ref[half:, :] = stacked([*pieces(bias), *pieces(diagonal)], PAD)


def transform_kernel(slots, members, *refs):
    part_refs, (place_ref, own_ref), out_refs = refs[:-4], refs[-4:-2], refs[-2:]
    half, row, column = triangles(members)
    packed, bias, diagonal = total_of(half, part_refs)
    corner, side = packed[:, :half], packed[:, half:]
    mirror = jnp.transpose(corner)
    first = jnp.where(row >= column, corner, mirror)
    last = jnp.where(
        row < column, corner, jnp.where(row == column, diagonal[:, :half], mirror)
    )
    gram = jnp.concatenate(
        [
            jnp.concatenate([first, side], axis=1),
            jnp.concatenate([jnp.transpose(side), last], axis=1),
        ],
        axis=0,
    )
    trace = jnp.sum(
        jnp.sum(jnp.where(row == column, first + last, 0.0), axis=0, keepdims=True),
        axis=1, keepdims=True,
    )
    scaling = float(members) / trace
    scaled = (gram * scaling).astype(BF16)
    bias = (bias * scaling).astype(BF16).astype(F32)

    def times(left):
        return jnp.dot(left, scaled, preferred_element_type=F32)

    first_power = times(jnp.concatenate([scaled, stacked([bias], PAD)], axis=0))
    square = first_power[:members].astype(BF16)
    bias_1 = first_power[members : members + 1]
    second_power = times(jnp.concatenate([square, stacked(pieces(bias_1), PAD)], axis=0))
    cubed = second_power[:members]
    bias_2 = joined(second_power[members:], 0)
    bias_3 = joined(times(stacked(pieces(bias_2), PAD)), 0)
    shift = bias - 0.5 * bias_1 + 0.375 * bias_2 - 0.3125 * bias_3
    identity = lax.broadcasted_iota(jnp.int32, (members, members), 0) == (
        lax.broadcasted_iota(jnp.int32, (members, members), 1)
    )
    transform = (
        jnp.where(identity, 1.0, 0.0)
        - 0.5 * scaled.astype(F32)
        + 0.375 * square.astype(F32)
        - 0.3125 * cubed
    ).astype(BF16)
    shift = stacked(pieces(shift), PAD)
    for side, out_ref in enumerate(out_refs):
        rows = jnp.dot(own_ref[side], transform, preferred_element_type=F32).astype(BF16)
        left = jnp.concatenate([rows, shift], axis=0)
        for index in range(out_ref.shape[1] // slots):
            step = index if side else 2 * index
            place = place_ref[:, step * slots : (step + 1) * slots]
            out_ref[:, index * slots : (index + 1) * slots] = jnp.dot(
                left, place, preferred_element_type=F32
            ).astype(BF16)


def own_means_of(slots, members, counts_ref, rank, seen_refs, cells):
    share = seen_refs[0].shape[1]
    own_means, mean = [], 0.0
    for step, ref in enumerate(seen_refs):
        packed = ref[slots:, :]
        row = jnp.concatenate(
            [joined(packed, 3 + 3 * index) for index in range(cells // share)], axis=1
        )
        own_means.append(row)
        mean = mean + row * as_row(counts_ref[rank ^ step], cells)
    return own_means, mean * (1.0 / members)


def product_kernel(slots, members, runners, plan, stride, counts_ref, rank_ref, left_ref, *refs):
    seen_refs, refs = refs[:runners], refs[runners:]
    cell_refs, out_refs = refs[: -len(plan)], refs[-len(plan) :]
    width = out_refs[0].shape[1]
    own_means, mean = own_means_of(
        slots, members, counts_ref, rank_ref[0], seen_refs, width * PARTS
    )
    lefts, sums = {}, {}
    for step in range(0, runners, stride):
        first = step // stride * slots
        lefts[step] = left_ref[:, first : first + slots]
        sums[step] = jnp.sum(lefts[step].astype(F32), axis=1, keepdims=True)
    place = 0
    for (part, steps), out_ref in zip(plan, out_refs):
        span = slice(part * width, (part + 1) * width)
        total = 0.0
        for step in steps:
            total = total + jnp.dot(
                lefts[step], cell_refs[place][...], preferred_element_type=F32
            )
            total = total + sums[step] * (own_means[step] - mean)[:, span]
            place = place + 1
        shift = joined(total[slots:], 0)
        if stride == 1:
            shift = shift + mean[:, span]
        out_ref[...] = (total[:slots] + shift).astype(out_ref.dtype)


def final_kernel(slots, rows, counts_ref, rank_ref, *refs):
    own_refs, refs = refs[:PARTS], refs[PARTS:]
    other_refs, (out_hbm, out_ref, sems) = refs[:-3], refs[-3:]
    columns = out_ref.shape[1]
    count = counts_ref[rank_ref[0]]
    chunk = slots // WRITES
    copies = []
    for index in range(WRITES):
        start = index * chunk
        live = lax.broadcasted_iota(jnp.int32, (chunk, columns), 0) + start < count
        row = 0
        for part, own_ref in enumerate(own_refs):
            for first in range(0, own_ref.shape[1], columns):
                span = slice(first, first + columns)
                total = own_ref[start : start + chunk, span]
                if part >= GATHERED:
                    other = other_refs[part - GATHERED][start : start + chunk, span]
                    total = total + other.astype(F32)
                out_ref[pl.ds(start * rows + row, chunk, stride=rows), :] = jnp.where(
                    live, total, 0.0
                )
                row = row + 1
        span = pl.ds(start * rows, chunk * rows)
        copies.append(
            pltpu.make_async_copy(out_ref.at[span], out_hbm.at[span], sems.at[index])
        )
        copies[-1].start()
    for copy in copies:
        copy.wait()


def body(states, diffusivity, velocity, counts, obs_index, obs_value, obs_weight):
    runners = lax.axis_size("runner")
    blocks = lax.axis_size("cells")
    slots, rows, columns = states.shape
    members = slots // 2 * runners
    half = members // 2
    cells = rows * columns
    seen = obs_index.shape[0]
    shares = 2
    share = seen // shares
    height = slots + PAD
    shape = jax.ShapeDtypeStruct

    rank = lax.axis_index("runner").astype(jnp.int32).reshape(1)
    last, first, flat, fields = call(
        functools.partial(edge_kernel, slots, rows),
        [shape((STEPS, height, columns), BF16)] * 2
        + [shape((slots * rows, columns), F32), shape((3, rows, columns), F32)],
        [],
        [states.reshape(slots * rows, columns), diffusivity, velocity],
        [pltpu.SemaphoreType.DMA((3,))],
        outside=True,
    )
    forward = [(i, (i + 1) % blocks) for i in range(blocks)]
    backward = [(target, source) for source, target in forward]
    low = lax.ppermute(last, "cells", forward)
    high = lax.ppermute(first, "cells", backward)
    pick, both, place, own = call(
        functools.partial(setup_kernel, slots, runners, members, shares),
        [
            shape((cells, seen), BF16),
            shape((8, share), F32),
            shape((members, runners * slots), BF16),
            shape((2, slots, members), BF16),
        ],
        [counts, rank],
        [obs_index[None, :], obs_value[None, :], obs_weight[None, :]],
    )

    coefs, inner = call(
        functools.partial(inner_kernel, slots, rows),
        [
            shape((rows, 5, 8, columns), F32),
            shape((sum(len(inside) for inside in inner_rows(rows)), slots, columns), F32),
        ],
        [],
        [flat, fields],
    )
    lower = -(-(3 + 3 * (cells // share)) // PAD) * PAD
    kept, given, *own_cells = call(
        functools.partial(forecast_kernel, slots, rows, shares),
        [shape((slots + lower, share), BF16)] * shares
        + [shape((slots, cells // PARTS), BF16)] * PARTS,
        [counts, rank],
        [flat, low, high, coefs, inner, pick],
        [
            pltpu.VMEM((rows + 2 * STEPS, 5, 8, columns), F32),
            pltpu.VMEM((rows, slots, columns), F32),
            pltpu.VMEM((height, cells), BF16),
        ],
    )

    def moved(array, runner_bit, block_bit=0):
        count = runners * blocks
        step = runner_bit * blocks + block_bit
        return lax.ppermute(array, ("runner", "cells"), partners(count, step))

    all_seen = [kept] + [
        moved(given if step % shares else kept, step)
        for step in range(1, runners)
    ]
    all_cells = {0: own_cells}
    bit = runners // 2
    while bit > 1:
        for step in list(all_cells):
            all_cells[step + bit] = [moved(array, bit) for array in all_cells[step]]
        bit = bit // 2
    even = sorted(all_cells)
    for part in range(GATHERED):
        for step in even:
            all_cells.setdefault(step + 1, []).append(moved(all_cells[step][part], 1))

    part = call(
        functools.partial(gram_kernel, slots, runners, members),
        shape((half + PAD, members), BF16),
        [counts, rank],
        [*all_seen, both, place],
    )
    stages = [[(0, 1)], [(1, 0)]]
    width = 2
    while width < blocks:
        reach = min(4, blocks // width)
        stages.append([(0, width * step) for step in reversed(range(1, reach))])
        width = width * reach
    for index, stage in enumerate(stages):
        parts = [part] + [moved(part, r, c) for r, c in stage]
        if index + 1 < len(stages):
            part = call(
                functools.partial(sum_kernel, half),
                shape((half + PAD, members), BF16),
                [],
                parts,
            )
    give, keep = call(
        functools.partial(transform_kernel, slots, members),
        [
            shape((height, runners // 2 * slots), BF16),
            shape((height, runners * slots), BF16),
        ],
        [],
        [*parts, place, own],
    )

    def product(left, plan, stride, dtype):
        return call(
            functools.partial(product_kernel, slots, members, runners, plan, stride),
            [shape((slots, cells // PARTS), dtype)] * len(plan),
            [counts, rank],
            [left, *all_seen] + [all_cells[step][part] for part, steps in plan for step in steps],
        )

    shared = [(part, even) for part in range(GATHERED, PARTS)]
    other_products = [moved(array, 1) for array in product(give, shared, 2, BF16)]
    whole = [(part, sorted(all_cells)) for part in range(GATHERED)]
    own_products = product(keep, whole + shared, 1, F32)
    analysed = call(
        functools.partial(final_kernel, slots, rows),
        shape((slots * rows, columns), F32),
        [counts, rank],
        [*own_products, *other_products],
        [pltpu.VMEM((slots * rows, columns), F32), pltpu.SemaphoreType.DMA((WRITES,))],
        write=True,
    )
    return analysed.reshape(slots, rows, columns)


def solution(mesh):
    return jax.shard_map(
        body,
        mesh=mesh,
        in_specs=(
            P("runner", "cells", None),
            P("cells", None),
            P(None, "cells", None),
            P(),
            P("cells"),
            P("cells"),
            P("cells"),
        ),
        out_specs=P("runner", "cells", None),
        check_vma=False,
    )
```

```python
import functools

import jax
import jax.numpy as jnp
from jax import lax
from jax.experimental import pallas as pl
from jax.experimental.pallas import tpu as pltpu
from jax.sharding import PartitionSpec as P


STEPS = 4
PAD = 16
F32 = jnp.float32
BF16 = jnp.bfloat16

PARTS = 2
WRITES = 4
GATHERED = 1


def partners(count, step):
    return [(i, i ^ step) for i in range(count)]


def pieces(row):
    high = row.astype(BF16).astype(F32)
    rest = row - high
    middle = rest.astype(BF16).astype(F32)
    return high, middle, rest - middle


def stacked(rows, height, dtype=BF16):
    width = rows[0].shape[1]
    place = lax.broadcasted_iota(jnp.int32, (height, width), 0)
    total = jnp.zeros((height, width), F32)
    for index, row in enumerate(rows):
        total = jnp.where(place == index, row, total)
    return total.astype(dtype)


def joined(block, first):
    block = block.astype(F32)
    return block[first : first + 1] + block[first + 1 : first + 2] + block[first + 2 : first + 3]


def offset_of(counts_ref, runner, runners):
    total = jnp.int32(0)
    for index in range(runners):
        total = total + jnp.where(index < runner, counts_ref[index], 0)
    return total


def count_row(table_ref, step, width):
    return jnp.tile(table_ref[step : step + 1, :], (1, width // table_ref.shape[1]))


def size_of(shape):
    size = shape.dtype.itemsize
    for extent in shape.shape:
        size = size * extent
    return size


def call(kernel, out_shape, scalars, vectors, scratch=(), outside=False, write=False):
    vector = pl.BlockSpec(memory_space=pltpu.VMEM)
    scalar = pl.BlockSpec(memory_space=pltpu.SMEM)
    hbm = pl.BlockSpec(memory_space=pltpu.HBM)
    if outside:
        vectors = [pltpu.with_memory_space_constraint(array, pltpu.HBM) for array in vectors]
    many = isinstance(out_shape, list)
    shapes = list(vectors) + (out_shape if many else [out_shape])
    held = sum(size_of(shape) for shape in shapes)
    return pl.pallas_call(
        kernel,
        out_shape=out_shape,
        in_specs=[scalar] * len(scalars) + [hbm if outside else vector] * len(vectors),
        out_specs=hbm if write else [vector] * len(out_shape) if many else vector,
        scratch_shapes=list(scratch),
        compiler_params=pltpu.CompilerParams(
            vmem_limit_bytes=min(56 << 20, (12 << 20) + 3 * held)
        ),
        cost_estimate=pl.CostEstimate(flops=0, bytes_accessed=1 << 20, transcendentals=0),
    )(*scalars, *vectors)


def edge_kernel(
    slots, rows, states_hbm, diff_hbm, vel_hbm, last_ref, first_ref, states_ref, fields_ref, sems
):
    copies = [
        pltpu.make_async_copy(states_hbm, states_ref, sems.at[0]),
        pltpu.make_async_copy(diff_hbm, fields_ref.at[0], sems.at[1]),
        pltpu.make_async_copy(vel_hbm, fields_ref.at[pl.ds(1, 2)], sems.at[2]),
    ]
    for copy in copies:
        copy.start()
    for copy in copies:
        copy.wait()
    for out_ref, base in ((last_ref, rows - STEPS), (first_ref, 0)):
        for j in range(STEPS):
            row = base + j
            out_ref[j, :slots, :] = states_ref[pl.ds(row, slots, stride=rows), :].astype(BF16)
            packed = []
            for field in range(3):
                packed.extend(pieces(fields_ref[field, row : row + 1]))
            out_ref[j, slots:, :] = stacked(packed, PAD)


def coefficients(diff, along, across):
    columns = diff.shape[1]
    return [
        jnp.broadcast_to(coef, (8, columns))
        for coef in (
            1.0 - 4.0 * diff,
            diff - 0.5 * along,
            diff + 0.5 * along,
            diff - 0.5 * across,
            diff + 0.5 * across,
        )
    ]


def advanced(u, above, below, coefs):
    columns = u.shape[1]
    return (
        u * (coefs[0] - 0.05 * (u * u))
        + coefs[1] * above
        + coefs[2] * below
        + coefs[3] * pltpu.roll(u, columns - 1, 1)
        + coefs[4] * pltpu.roll(u, 1, 1)
    )


def inner_rows(rows):
    return [range(step, rows - step) for step in range(1, STEPS) if step < rows - step]


def inner_kernel(slots, rows, states_ref, fields_ref, coef_ref, inner_ref):
    for row in range(rows):
        fields = [fields_ref[field, row : row + 1] for field in range(3)]
        for index, coef in enumerate(coefficients(*fields)):
            coef_ref[row, index] = coef
    for start in range(0, slots, 16):
        values = []
        for row in range(rows):
            block = states_ref[pl.ds(start * rows + row, 16, stride=rows), :]
            values.append([block[8 * h : 8 * h + 8] for h in range(2)])
        place = 0
        for inside in inner_rows(rows):
            after = list(values)
            for row in inside:
                coefs = [coef_ref[row, index] for index in range(5)]
                after[row] = [
                    advanced(values[row][h], values[row + 1][h], values[row - 1][h], coefs)
                    for h in range(2)
                ]
                for h in range(2):
                    inner_ref[place, start + 8 * h : start + 8 * h + 8, :] = after[row][h]
                place = place + 1
            values = after


def forecast_kernel(
    slots, rows, shares, table_ref, states_ref, low_ref, high_ref, own_coef_ref, inner_ref,
    pick_ref, *rest,
):
    (coef_ref, value_ref, cells_ref) = rest[-3:]
    seen_refs, part_refs = rest[:shares], rest[shares:-3]
    columns = states_ref.shape[1]
    total_rows = rows + 2 * STEPS
    count = count_row(table_ref, 0, columns)

    for row in [*range(1, STEPS), *range(STEPS + rows, total_rows - 1)]:
        block = (low_ref[row] if row < STEPS else high_ref[row - STEPS - rows])[slots:]
        fields = [joined(block, 3 * field) for field in range(3)]
        for index, coef in enumerate(coefficients(*fields)):
            coef_ref[row, index] = coef

    known = {}
    for step, inside in enumerate(inner_rows(rows)):
        for row in inside:
            known[step, row + STEPS] = len(known)
    chunk = 16
    halves = chunk // 8
    sums = [jnp.zeros((8, columns), F32)] * rows
    for start in range(0, slots, chunk):
        values = []
        for row in range(total_rows):
            if row < STEPS:
                block = low_ref[row, start : start + chunk, :].astype(F32)
            elif row < STEPS + rows:
                block = states_ref[pl.ds(start * rows + row - STEPS, chunk, stride=rows), :]
            else:
                block = high_ref[row - STEPS - rows, start : start + chunk, :].astype(F32)
            values.append([block[8 * h : 8 * h + 8] for h in range(halves)])
        for step in range(STEPS):
            after = list(values)
            for row in range(step + 1, total_rows - step - 1):
                if (step, row) in known:
                    block = inner_ref[known[step, row], start : start + chunk, :]
                    after[row] = [block[8 * h : 8 * h + 8] for h in range(halves)]
                    continue
                if STEPS <= row < STEPS + rows:
                    coefs = [own_coef_ref[row - STEPS, index] for index in range(5)]
                else:
                    coefs = [coef_ref[row, index] for index in range(5)]
                after[row] = [
                    advanced(values[row][h], values[row + 1][h], values[row - 1][h], coefs)
                    for h in range(halves)
                ]
            values = after
        for h in range(halves):
            place = lax.broadcasted_iota(jnp.int32, (8, columns), 0) + (start + 8 * h)
            live = place.astype(F32) < count
            for row in range(rows):
                u = jnp.where(live, values[row + STEPS][h], 0.0)
                sums[row] = sums[row] + u
                value_ref[row, start + 8 * h : start + 8 * h + 8, :] = u

    live = lax.broadcasted_iota(jnp.int32, (slots, columns), 0).astype(F32) < count
    inverse = 1.0 / count
    means = []
    for row in range(rows):
        mean = jnp.sum(sums[row], axis=0, keepdims=True) * inverse
        part = jnp.where(live, value_ref[row] - mean, 0.0).astype(BF16)
        cells_ref[:slots, row * columns : (row + 1) * columns] = part
        cells_ref[slots:, row * columns : (row + 1) * columns] = stacked(pieces(mean), PAD)
        means.append(mean)
    width = rows * columns // len(part_refs)
    for index, part_ref in enumerate(part_refs):
        part_ref[...] = cells_ref[:slots, index * width : (index + 1) * width]
    seen = jnp.dot(cells_ref[...], pick_ref[...], preferred_element_type=F32)
    share = seen.shape[1] // shares
    packed = [jnp.zeros((1, share), F32)] * 3
    for first in range(0, rows, share // columns):
        packed.extend(
            pieces(jnp.concatenate(means[first : first + share // columns], axis=1))
        )
    packed = stacked(packed, seen_refs[0].shape[0] - slots)
    for index, seen_ref in enumerate(seen_refs):
        part = seen[:, index * share : (index + 1) * share].astype(BF16)
        seen_ref[:slots, :] = part[:slots]
        seen_ref[slots : slots + PAD, :] = part[slots:] + packed[:PAD]
        if packed.shape[0] > PAD:
            seen_ref[slots + PAD :, :] = packed[PAD:]


def placing(slots, runners, members, counts_ref, runner, by_slot):
    shape, slot_dim = ((slots, members), 0) if by_slot else ((members, slots), 1)
    slot = lax.broadcasted_iota(jnp.int32, shape, slot_dim)
    member = lax.broadcasted_iota(jnp.int32, shape, 1 - slot_dim)
    offset = offset_of(counts_ref, runner, runners)
    hit = (member - slot == offset) & (slot < counts_ref[runner])
    return jnp.where(hit, 1.0, 0.0).astype(BF16)


def setup_kernel(
    slots, runners, members, shares, counts_ref, rank_ref, index_ref, value_ref, weight_ref,
    pick_ref, seen_ref, place_ref, own_ref, table_ref,
):
    rank = rank_ref[0]
    share = index_ref.shape[1] // shares

    def own_first(ref):
        swapped = jnp.concatenate([ref[:, share:], ref[:, :share]], axis=1)
        return jnp.where(jnp.bitwise_and(rank, 1) == 0, ref[...], swapped)

    wanted = own_first(index_ref)
    cell = lax.broadcasted_iota(jnp.int32, pick_ref.shape, 0)
    pick_ref[...] = jnp.where(cell == wanted, 1.0, 0.0).astype(BF16)
    seen_ref[...] = stacked([own_first(value_ref)[:, :share], own_first(weight_ref)[:, :share]], 8, F32)
    for step in range(runners):
        place_ref[:, step * slots : (step + 1) * slots] = placing(
            slots, runners, members, counts_ref, rank ^ step, False
        )
        count = jnp.full((1, table_ref.shape[1]), counts_ref[rank ^ step], jnp.int32)
        table_ref[step : step + 1, :] = count.astype(F32)
    for side in range(2):
        own_ref[side] = placing(slots, runners, members, counts_ref, rank ^ (1 - side), True)


def triangles(members):
    half = members // 2
    row = lax.broadcasted_iota(jnp.int32, (half, half), 0)
    column = lax.broadcasted_iota(jnp.int32, (half, half), 1)
    return half, row, column


def gram_kernel(slots, runners, members, *refs):
    seen_refs, (table_ref, both_ref, place_ref, out_ref) = refs[:runners], refs[runners:]
    own_means = [joined(ref[slots:, :], 0) for ref in seen_refs]
    width = both_ref.shape[1]
    mean = 0.0
    for step, row in enumerate(own_means):
        mean = mean + row * count_row(table_ref, step, width)
    mean = mean * (1.0 / members)
    observed = 0.0
    for step, ref in enumerate(seen_refs):
        part = ref[:slots, :].astype(F32) + (own_means[step] - mean)
        place = place_ref[:, step * slots : (step + 1) * slots]
        observed = observed + jnp.dot(place, part.astype(BF16), preferred_element_type=F32)
    weighted = (observed * both_ref[1:2, :]).astype(BF16)
    across = (((1,), (1,)), ((), ()))
    gram = lax.dot_general(
        weighted, observed.astype(BF16), across, preferred_element_type=F32
    )
    innovation = stacked(pieces(both_ref[0:1, :] - mean), PAD)
    bias = lax.dot_general(innovation, weighted, across, preferred_element_type=F32)
    half, row, column = triangles(members)
    last = gram[half:, half:]
    out_ref[:half, :half] = jnp.where(row >= column, gram[:half, :half], last).astype(BF16)
    out_ref[:half, half:] = gram[:half, half:].astype(BF16)
    diagonal = jnp.sum(jnp.where(row == column, last, 0.0), axis=0, keepdims=True)
    diagonal = jnp.concatenate([diagonal, jnp.zeros_like(diagonal)], axis=1)
    out_ref[half:, :] = stacked([*pieces(joined(bias, 0)), *pieces(diagonal)], PAD)


def total_of(half, part_refs):
    packed, bias, diagonal = 0.0, 0.0, 0.0
    for ref in part_refs:
        packed = packed + ref[:half, :].astype(F32)
        bias = bias + joined(ref[half:, :], 0)
        diagonal = diagonal + joined(ref[half:, :], 3)
    return packed, bias, diagonal


def sum_kernel(half, *refs):
    part_refs, out_ref = refs[:-1], refs[-1]
    packed, bias, diagonal = total_of(half, part_refs)
    out_ref[:half, :] = packed.astype(BF16)
    out_ref[half:, :] = stacked([*pieces(bias), *pieces(diagonal)], PAD)


def transform_kernel(slots, members, *refs):
    part_refs, (place_ref, own_ref), out_refs = refs[:-4], refs[-4:-2], refs[-2:]
    half, row, column = triangles(members)
    packed, bias, diagonal = total_of(half, part_refs)
    corner, side = packed[:, :half], packed[:, half:]
    mirror = jnp.transpose(corner)
    first = jnp.where(row >= column, corner, mirror)
    last = jnp.where(
        row < column, corner, jnp.where(row == column, diagonal[:, :half], mirror)
    )
    gram = jnp.concatenate(
        [
            jnp.concatenate([first, side], axis=1),
            jnp.concatenate([jnp.transpose(side), last], axis=1),
        ],
        axis=0,
    )
    trace = jnp.sum(
        jnp.sum(jnp.where(row == column, first + last, 0.0), axis=0, keepdims=True),
        axis=1, keepdims=True,
    )
    scaling = float(members) / trace
    scaled = (gram * scaling).astype(BF16)
    bias = (bias * scaling).astype(BF16).astype(F32)

    def times(left):
        return jnp.dot(left, scaled, preferred_element_type=F32)

    first_power = times(jnp.concatenate([scaled, stacked([bias], PAD)], axis=0))
    square = first_power[:members].astype(BF16)
    bias_1 = first_power[members : members + 1]
    second_power = times(jnp.concatenate([square, stacked(pieces(bias_1), PAD)], axis=0))
    cubed = second_power[:members]
    bias_2 = joined(second_power[members:], 0)
    bias_3 = joined(times(stacked(pieces(bias_2), PAD)), 0)
    shift = bias - 0.5 * bias_1 + 0.375 * bias_2 - 0.3125 * bias_3
    identity = lax.broadcasted_iota(jnp.int32, (members, members), 0) == (
        lax.broadcasted_iota(jnp.int32, (members, members), 1)
    )
    transform = (
        jnp.where(identity, 1.0, 0.0)
        - 0.5 * scaled.astype(F32)
        + 0.375 * square.astype(F32)
        - 0.3125 * cubed
    ).astype(BF16)
    shift = stacked(pieces(shift), PAD)
    for side, out_ref in enumerate(out_refs):
        rows = jnp.dot(own_ref[side], transform, preferred_element_type=F32).astype(BF16)
        left = jnp.concatenate([rows, shift], axis=0)
        for index in range(out_ref.shape[1] // slots):
            step = index if side else 2 * index
            place = place_ref[:, step * slots : (step + 1) * slots]
            out_ref[:, index * slots : (index + 1) * slots] = jnp.dot(
                left, place, preferred_element_type=F32
            ).astype(BF16)


def own_means_of(slots, members, table_ref, seen_refs, cells):
    share = seen_refs[0].shape[1]
    own_means, mean = [], 0.0
    for step, ref in enumerate(seen_refs):
        packed = ref[slots:, :]
        row = jnp.concatenate(
            [joined(packed, 3 + 3 * index) for index in range(cells // share)], axis=1
        )
        own_means.append(row)
        mean = mean + row * count_row(table_ref, step, cells)
    return own_means, mean * (1.0 / members)


def product_kernel(slots, members, runners, plan, stride, table_ref, left_ref, *refs):
    seen_refs, refs = refs[:runners], refs[runners:]
    cell_refs, out_refs = refs[: -len(plan)], refs[-len(plan) :]
    width = out_refs[0].shape[1]
    own_means, mean = own_means_of(
        slots, members, table_ref, seen_refs, width * PARTS
    )
    lefts, sums = {}, {}
    for step in range(0, runners, stride):
        first = step // stride * slots
        lefts[step] = left_ref[:, first : first + slots]
        sums[step] = jnp.sum(lefts[step].astype(F32), axis=1, keepdims=True)
    place = 0
    for (part, steps), out_ref in zip(plan, out_refs):
        span = slice(part * width, (part + 1) * width)
        total = 0.0
        for step in steps:
            total = total + jnp.dot(
                lefts[step], cell_refs[place][...], preferred_element_type=F32
            )
            total = total + sums[step] * (own_means[step] - mean)[:, span]
            place = place + 1
        shift = joined(total[slots:], 0)
        if stride == 1:
            shift = shift + mean[:, span]
        out_ref[...] = (total[:slots] + shift).astype(out_ref.dtype)


def final_kernel(slots, rows, table_ref, *refs):
    own_refs, refs = refs[:PARTS], refs[PARTS:]
    other_refs, (out_hbm, out_ref, sems) = refs[:-3], refs[-3:]
    columns = out_ref.shape[1]
    count = count_row(table_ref, 0, columns)
    chunk = slots // WRITES
    copies = []
    for index in range(WRITES):
        start = index * chunk
        slot = lax.broadcasted_iota(jnp.int32, (chunk, columns), 0) + start
        live = slot.astype(F32) < count
        row = 0
        for part, own_ref in enumerate(own_refs):
            for first in range(0, own_ref.shape[1], columns):
                span = slice(first, first + columns)
                total = own_ref[start : start + chunk, span]
                if part >= GATHERED:
                    other = other_refs[part - GATHERED][start : start + chunk, span]
                    total = total + other.astype(F32)
                out_ref[pl.ds(start * rows + row, chunk, stride=rows), :] = jnp.where(
                    live, total, 0.0
                )
                row = row + 1
        span = pl.ds(start * rows, chunk * rows)
        copies.append(
            pltpu.make_async_copy(out_ref.at[span], out_hbm.at[span], sems.at[index])
        )
        copies[-1].start()
    for copy in copies:
        copy.wait()


def body(states, diffusivity, velocity, counts, obs_index, obs_value, obs_weight):
    runners = lax.axis_size("runner")
    blocks = lax.axis_size("cells")
    slots, rows, columns = states.shape
    members = slots // 2 * runners
    half = members // 2
    cells = rows * columns
    seen = obs_index.shape[0]
    shares = 2
    share = seen // shares
    height = slots + PAD
    shape = jax.ShapeDtypeStruct

    rank = lax.axis_index("runner").astype(jnp.int32).reshape(1)
    last, first, flat, fields = call(
        functools.partial(edge_kernel, slots, rows),
        [shape((STEPS, height, columns), BF16)] * 2
        + [shape((slots * rows, columns), F32), shape((3, rows, columns), F32)],
        [],
        [states.reshape(slots * rows, columns), diffusivity, velocity],
        [pltpu.SemaphoreType.DMA((3,))],
        outside=True,
    )
    forward = [(i, (i + 1) % blocks) for i in range(blocks)]
    backward = [(target, source) for source, target in forward]
    low = lax.ppermute(last, "cells", forward)
    high = lax.ppermute(first, "cells", backward)
    pick, both, place, own, table = call(
        functools.partial(setup_kernel, slots, runners, members, shares),
        [
            shape((cells, seen), BF16),
            shape((8, share), F32),
            shape((members, runners * slots), BF16),
            shape((2, slots, members), BF16),
            shape((runners, columns), F32),
        ],
        [counts, rank],
        [obs_index[None, :], obs_value[None, :], obs_weight[None, :]],
    )

    coefs, inner = call(
        functools.partial(inner_kernel, slots, rows),
        [
            shape((rows, 5, 8, columns), F32),
            shape((sum(len(inside) for inside in inner_rows(rows)), slots, columns), F32),
        ],
        [],
        [flat, fields],
    )
    lower = -(-(3 + 3 * (cells // share)) // PAD) * PAD
    kept, given, *own_cells = call(
        functools.partial(forecast_kernel, slots, rows, shares),
        [shape((slots + lower, share), BF16)] * shares
        + [shape((slots, cells // PARTS), BF16)] * PARTS,
        [],
        [table, flat, low, high, coefs, inner, pick],
        [
            pltpu.VMEM((rows + 2 * STEPS, 5, 8, columns), F32),
            pltpu.VMEM((rows, slots, columns), F32),
            pltpu.VMEM((height, cells), BF16),
        ],
    )

    def moved(array, runner_bit, block_bit=0):
        count = runners * blocks
        step = runner_bit * blocks + block_bit
        return lax.ppermute(array, ("runner", "cells"), partners(count, step))

    all_seen = [kept] + [
        moved(given if step % shares else kept, step)
        for step in range(1, runners)
    ]
    all_cells = {0: own_cells}
    bit = runners // 2
    while bit > 1:
        for step in list(all_cells):
            all_cells[step + bit] = [moved(array, bit) for array in all_cells[step]]
        bit = bit // 2
    even = sorted(all_cells)
    for part in range(GATHERED):
        for step in even:
            all_cells.setdefault(step + 1, []).append(moved(all_cells[step][part], 1))

    part = call(
        functools.partial(gram_kernel, slots, runners, members),
        shape((half + PAD, members), BF16),
        [],
        [*all_seen, table, both, place],
    )
    stages = [[(0, 1)], [(1, 0)]]
    width = 2
    while width < blocks:
        reach = min(4, blocks // width)
        stages.append([(0, width * step) for step in reversed(range(1, reach))])
        width = width * reach
    for index, stage in enumerate(stages):
        parts = [part] + [moved(part, r, c) for r, c in stage]
        if index + 1 < len(stages):
            part = call(
                functools.partial(sum_kernel, half),
                shape((half + PAD, members), BF16),
                [],
                parts,
            )
    give, keep = call(
        functools.partial(transform_kernel, slots, members),
        [
            shape((height, runners // 2 * slots), BF16),
            shape((height, runners * slots), BF16),
        ],
        [],
        [*parts, place, own],
    )

    def product(left, plan, stride, dtype):
        return call(
            functools.partial(product_kernel, slots, members, runners, plan, stride),
            [shape((slots, cells // PARTS), dtype)] * len(plan),
            [],
            [table, left, *all_seen] + [all_cells[step][part] for part, steps in plan for step in steps],
        )

    shared = [(part, even) for part in range(GATHERED, PARTS)]
    other_products = [moved(array, 1) for array in product(give, shared, 2, BF16)]
    whole = [(part, sorted(all_cells)) for part in range(GATHERED)]
    own_products = product(keep, whole + shared, 1, F32)
    analysed = call(
        functools.partial(final_kernel, slots, rows),
        shape((slots * rows, columns), F32),
        [],
        [table, *own_products, *other_products],
        [pltpu.VMEM((slots * rows, columns), F32), pltpu.SemaphoreType.DMA((WRITES,))],
        write=True,
    )
    return analysed.reshape(slots, rows, columns)


def solution(mesh):
    return jax.shard_map(
        body,
        mesh=mesh,
        in_specs=(
            P("runner", "cells", None),
            P("cells", None),
            P(None, "cells", None),
            P(),
            P("cells"),
            P("cells"),
            P("cells"),
        ),
        out_specs=P("runner", "cells", None),
        check_vma=False,
    )
```

```python
import functools

import jax
import jax.numpy as jnp
from jax import lax
from jax.experimental import pallas as pl
from jax.experimental.pallas import tpu as pltpu
from jax.sharding import PartitionSpec as P


STEPS = 4
PAD = 16
F32 = jnp.float32
BF16 = jnp.bfloat16

PARTS = 2
WRITES = 4
GATHERED = 1


def partners(count, step):
    return [(i, i ^ step) for i in range(count)]


def pieces(row):
    high = row.astype(BF16).astype(F32)
    rest = row - high
    middle = rest.astype(BF16).astype(F32)
    return high, middle, rest - middle


def stacked(rows, height, dtype=BF16):
    width = rows[0].shape[1]
    place = lax.broadcasted_iota(jnp.int32, (height, width), 0)
    total = jnp.zeros((height, width), F32)
    for index, row in enumerate(rows):
        total = jnp.where(place == index, row, total)
    return total.astype(dtype)


def joined(block, first):
    block = block.astype(F32)
    return block[first : first + 1] + block[first + 1 : first + 2] + block[first + 2 : first + 3]


def offset_of(counts_ref, runner, runners):
    total = jnp.int32(0)
    for index in range(runners):
        total = total + jnp.where(index < runner, counts_ref[index], 0)
    return total


def count_row(table_ref, step, width):
    return jnp.tile(table_ref[step : step + 1, :], (1, width // table_ref.shape[1]))


def size_of(shape):
    size = shape.dtype.itemsize
    for extent in shape.shape:
        size = size * extent
    return size


def call(kernel, out_shape, scalars, vectors, scratch=(), outside=False, write=False):
    vector = pl.BlockSpec(memory_space=pltpu.VMEM)
    scalar = pl.BlockSpec(memory_space=pltpu.SMEM)
    hbm = pl.BlockSpec(memory_space=pltpu.HBM)
    if outside:
        vectors = [pltpu.with_memory_space_constraint(array, pltpu.HBM) for array in vectors]
    many = isinstance(out_shape, list)
    shapes = list(vectors) + (out_shape if many else [out_shape])
    held = sum(size_of(shape) for shape in shapes)
    return pl.pallas_call(
        kernel,
        out_shape=out_shape,
        in_specs=[scalar] * len(scalars) + [hbm if outside else vector] * len(vectors),
        out_specs=hbm if write else [vector] * len(out_shape) if many else vector,
        scratch_shapes=list(scratch),
        compiler_params=pltpu.CompilerParams(
            vmem_limit_bytes=min(56 << 20, (12 << 20) + 3 * held)
        ),
        cost_estimate=pl.CostEstimate(flops=0, bytes_accessed=1 << 20, transcendentals=0),
    )(*scalars, *vectors)


def edge_kernel(
    slots, rows, states_hbm, diff_hbm, vel_hbm, last_ref, first_ref, states_ref, fields_ref, sems
):
    copies = [
        pltpu.make_async_copy(states_hbm, states_ref, sems.at[0]),
        pltpu.make_async_copy(diff_hbm, fields_ref.at[0], sems.at[1]),
        pltpu.make_async_copy(vel_hbm, fields_ref.at[pl.ds(1, 2)], sems.at[2]),
    ]
    for copy in copies:
        copy.start()
    for copy in copies:
        copy.wait()
    for out_ref, base in ((last_ref, rows - STEPS), (first_ref, 0)):
        for j in range(STEPS):
            row = base + j
            out_ref[j, :slots, :] = states_ref[pl.ds(row, slots, stride=rows), :].astype(BF16)
            packed = []
            for field in range(3):
                packed.extend(pieces(fields_ref[field, row : row + 1]))
            out_ref[j, slots:, :] = stacked(packed, PAD)


def coefficients(diff, along, across):
    columns = diff.shape[1]
    return [
        jnp.broadcast_to(coef, (8, columns))
        for coef in (
            1.0 - 4.0 * diff,
            diff - 0.5 * along,
            diff + 0.5 * along,
            diff - 0.5 * across,
            diff + 0.5 * across,
        )
    ]


def advanced(u, above, below, coefs):
    columns = u.shape[1]
    return (
        u * (coefs[0] - 0.05 * (u * u))
        + coefs[1] * above
        + coefs[2] * below
        + coefs[3] * pltpu.roll(u, columns - 1, 1)
        + coefs[4] * pltpu.roll(u, 1, 1)
    )


def inner_rows(rows):
    return [range(step, rows - step) for step in range(1, STEPS) if step < rows - step]


def inner_kernel(slots, rows, states_ref, fields_ref, coef_ref, inner_ref):
    for row in range(rows):
        fields = [fields_ref[field, row : row + 1] for field in range(3)]
        for index, coef in enumerate(coefficients(*fields)):
            coef_ref[row, index] = coef
    for start in range(0, slots, 16):
        values = []
        for row in range(rows):
            block = states_ref[pl.ds(start * rows + row, 16, stride=rows), :]
            values.append([block[8 * h : 8 * h + 8] for h in range(2)])
        place = 0
        for inside in inner_rows(rows):
            after = list(values)
            for row in inside:
                coefs = [coef_ref[row, index] for index in range(5)]
                after[row] = [
                    advanced(values[row][h], values[row + 1][h], values[row - 1][h], coefs)
                    for h in range(2)
                ]
                for h in range(2):
                    inner_ref[place, start + 8 * h : start + 8 * h + 8, :] = after[row][h]
                place = place + 1
            values = after


def forecast_kernel(
    slots, rows, shares, table_ref, states_ref, low_ref, high_ref, own_coef_ref, inner_ref,
    pick_ref, *rest,
):
    (coef_ref, value_ref, cells_ref) = rest[-3:]
    seen_refs, part_refs = rest[:shares], rest[shares:-3]
    columns = states_ref.shape[1]
    total_rows = rows + 2 * STEPS
    count = count_row(table_ref, 0, columns)

    for row in [*range(1, STEPS), *range(STEPS + rows, total_rows - 1)]:
        block = (low_ref[row] if row < STEPS else high_ref[row - STEPS - rows])[slots:]
        fields = [joined(block, 3 * field) for field in range(3)]
        for index, coef in enumerate(coefficients(*fields)):
            coef_ref[row, index] = coef

    known = {}
    for step, inside in enumerate(inner_rows(rows)):
        for row in inside:
            known[step, row + STEPS] = len(known)
    chunk = 16
    halves = chunk // 8
    sums = [jnp.zeros((8, columns), F32)] * rows
    for start in range(0, slots, chunk):
        values = []
        for row in range(total_rows):
            if row < STEPS:
                block = low_ref[row, start : start + chunk, :].astype(F32)
            elif row < STEPS + rows:
                block = states_ref[pl.ds(start * rows + row - STEPS, chunk, stride=rows), :]
            else:
                block = high_ref[row - STEPS - rows, start : start + chunk, :].astype(F32)
            values.append([block[8 * h : 8 * h + 8] for h in range(halves)])
        for step in range(STEPS):
            after = list(values)
            for row in range(step + 1, total_rows - step - 1):
                if (step, row) in known:
                    block = inner_ref[known[step, row], start : start + chunk, :]
                    after[row] = [block[8 * h : 8 * h + 8] for h in range(halves)]
                    continue
                if STEPS <= row < STEPS + rows:
                    coefs = [own_coef_ref[row - STEPS, index] for index in range(5)]
                else:
                    coefs = [coef_ref[row, index] for index in range(5)]
                after[row] = [
                    advanced(values[row][h], values[row + 1][h], values[row - 1][h], coefs)
                    for h in range(halves)
                ]
            values = after
        for h in range(halves):
            place = lax.broadcasted_iota(jnp.int32, (8, columns), 0) + (start + 8 * h)
            live = place.astype(F32) < count
            for row in range(rows):
                u = jnp.where(live, values[row + STEPS][h], 0.0)
                sums[row] = sums[row] + u
                value_ref[row, start + 8 * h : start + 8 * h + 8, :] = u

    live = lax.broadcasted_iota(jnp.int32, (slots, columns), 0).astype(F32) < count
    inverse = 1.0 / count
    means = []
    for row in range(rows):
        mean = jnp.sum(sums[row], axis=0, keepdims=True) * inverse
        part = jnp.where(live, value_ref[row] - mean, 0.0).astype(BF16)
        cells_ref[:slots, row * columns : (row + 1) * columns] = part
        cells_ref[slots:, row * columns : (row + 1) * columns] = stacked(pieces(mean), PAD)
        means.append(mean)
    width = rows * columns // len(part_refs)
    for index, part_ref in enumerate(part_refs):
        part_ref[...] = cells_ref[:slots, index * width : (index + 1) * width]
    seen = jnp.dot(cells_ref[...], pick_ref[...], preferred_element_type=F32)
    share = seen.shape[1] // shares
    packed = [jnp.zeros((1, share), F32)] * 3
    for first in range(0, rows, share // columns):
        packed.extend(
            pieces(jnp.concatenate(means[first : first + share // columns], axis=1))
        )
    packed = stacked(packed, seen_refs[0].shape[0] - slots)
    for index, seen_ref in enumerate(seen_refs):
        part = seen[:, index * share : (index + 1) * share].astype(BF16)
        seen_ref[:slots, :] = part[:slots]
        seen_ref[slots : slots + PAD, :] = part[slots:] + packed[:PAD]
        if packed.shape[0] > PAD:
            seen_ref[slots + PAD :, :] = packed[PAD:]


def placing(slots, runners, members, counts_ref, runner, by_slot):
    shape, slot_dim = ((slots, members), 0) if by_slot else ((members, slots), 1)
    slot = lax.broadcasted_iota(jnp.int32, shape, slot_dim)
    member = lax.broadcasted_iota(jnp.int32, shape, 1 - slot_dim)
    offset = offset_of(counts_ref, runner, runners)
    hit = (member - slot == offset) & (slot < counts_ref[runner])
    return jnp.where(hit, 1.0, 0.0).astype(BF16)


def setup_kernel(
    slots, runners, members, shares, counts_ref, rank_ref, index_ref, value_ref, weight_ref,
    pick_ref, seen_ref, place_ref, own_ref, table_ref,
):
    rank = rank_ref[0]
    share = index_ref.shape[1] // shares

    def own_first(ref):
        swapped = jnp.concatenate([ref[:, share:], ref[:, :share]], axis=1)
        return jnp.where(jnp.bitwise_and(rank, 1) == 0, ref[...], swapped)

    wanted = own_first(index_ref)
    cell = lax.broadcasted_iota(jnp.int32, pick_ref.shape, 0)
    pick_ref[...] = jnp.where(cell == wanted, 1.0, 0.0).astype(BF16)
    seen_ref[...] = stacked([own_first(value_ref)[:, :share], own_first(weight_ref)[:, :share]], 8, F32)
    for step in range(runners):
        place_ref[:, step * slots : (step + 1) * slots] = placing(
            slots, runners, members, counts_ref, rank ^ step, False
        )
        count = jnp.full((1, table_ref.shape[1]), counts_ref[rank ^ step], jnp.int32)
        table_ref[step : step + 1, :] = count.astype(F32)
    for side in range(2):
        own_ref[side] = placing(slots, runners, members, counts_ref, rank ^ (1 - side), True)


def triangles(members):
    half = members // 2
    row = lax.broadcasted_iota(jnp.int32, (half, half), 0)
    column = lax.broadcasted_iota(jnp.int32, (half, half), 1)
    return half, row, column


def gram_kernel(slots, runners, members, *refs):
    seen_refs, (table_ref, both_ref, place_ref, out_ref) = refs[:runners], refs[runners:]
    own_means = [joined(ref[slots:, :], 0) for ref in seen_refs]
    width = both_ref.shape[1]
    mean = 0.0
    for step, row in enumerate(own_means):
        mean = mean + row * count_row(table_ref, step, width)
    mean = mean * (1.0 / members)
    observed = 0.0
    for step, ref in enumerate(seen_refs):
        part = ref[:slots, :].astype(F32) + (own_means[step] - mean)
        place = place_ref[:, step * slots : (step + 1) * slots]
        observed = observed + jnp.dot(place, part.astype(BF16), preferred_element_type=F32)
    weighted = (observed * both_ref[1:2, :]).astype(BF16)
    across = (((1,), (1,)), ((), ()))
    gram = lax.dot_general(
        weighted, observed.astype(BF16), across, preferred_element_type=F32
    )
    innovation = stacked(pieces(both_ref[0:1, :] - mean), PAD)
    bias = lax.dot_general(innovation, weighted, across, preferred_element_type=F32)
    half, row, column = triangles(members)
    last = gram[half:, half:]
    out_ref[:half, :half] = jnp.where(row >= column, gram[:half, :half], last).astype(BF16)
    out_ref[:half, half:] = gram[:half, half:].astype(BF16)
    diagonal = jnp.sum(jnp.where(row == column, last, 0.0), axis=0, keepdims=True)
    diagonal = jnp.concatenate([diagonal, jnp.zeros_like(diagonal)], axis=1)
    out_ref[half:, :] = stacked([*pieces(joined(bias, 0)), *pieces(diagonal)], PAD)


def total_of(half, part_refs):
    packed, bias, diagonal = 0.0, 0.0, 0.0
    for ref in part_refs:
        packed = packed + ref[:half, :].astype(F32)
        bias = bias + joined(ref[half:, :], 0)
        diagonal = diagonal + joined(ref[half:, :], 3)
    return packed, bias, diagonal


def sum_kernel(half, *refs):
    part_refs, out_ref = refs[:-1], refs[-1]
    packed, bias, diagonal = total_of(half, part_refs)
    out_ref[:half, :] = packed.astype(BF16)
    out_ref[half:, :] = stacked([*pieces(bias), *pieces(diagonal)], PAD)


def transform_kernel(slots, members, runners, sums, plan, *refs):
    part_refs, refs = refs[:sums], refs[sums:]
    (place_ref, own_ref, table_ref), refs = refs[:3], refs[3:]
    (transform_ref, shift_ref), refs = refs[-2:], refs[:-2]
    half, row, column = triangles(members)
    packed, bias, diagonal = total_of(half, part_refs)
    corner, side = packed[:, :half], packed[:, half:]
    mirror = jnp.transpose(corner)
    first = jnp.where(row >= column, corner, mirror)
    last = jnp.where(
        row < column, corner, jnp.where(row == column, diagonal[:, :half], mirror)
    )
    gram = jnp.concatenate(
        [
            jnp.concatenate([first, side], axis=1),
            jnp.concatenate([jnp.transpose(side), last], axis=1),
        ],
        axis=0,
    )
    trace = jnp.sum(
        jnp.sum(jnp.where(row == column, first + last, 0.0), axis=0, keepdims=True),
        axis=1, keepdims=True,
    )
    scaling = float(members) / trace
    scaled = (gram * scaling).astype(BF16)
    bias = (bias * scaling).astype(BF16).astype(F32)

    def times(left):
        return jnp.dot(left, scaled, preferred_element_type=F32)

    first_power = times(jnp.concatenate([scaled, stacked([bias], PAD)], axis=0))
    square = first_power[:members].astype(BF16)
    bias_1 = first_power[members : members + 1]
    second_power = times(jnp.concatenate([square, stacked(pieces(bias_1), PAD)], axis=0))
    cubed = second_power[:members]
    bias_2 = joined(second_power[members:], 0)
    bias_3 = joined(times(stacked(pieces(bias_2), PAD)), 0)
    shift = bias - 0.5 * bias_1 + 0.375 * bias_2 - 0.3125 * bias_3
    identity = lax.broadcasted_iota(jnp.int32, (members, members), 0) == (
        lax.broadcasted_iota(jnp.int32, (members, members), 1)
    )
    transform = (
        jnp.where(identity, 1.0, 0.0)
        - 0.5 * scaled.astype(F32)
        + 0.375 * square.astype(F32)
        - 0.3125 * cubed
    ).astype(BF16)
    shift = stacked(pieces(shift), PAD)
    transform_ref[...] = transform
    shift_ref[...] = shift
    write_products(
        slots, members, runners, plan, 0, transform, shift, own_ref, place_ref, table_ref, refs
    )


def keep_kernel(
    slots, members, runners, plan, transform_ref, shift_ref, own_ref, place_ref, table_ref, *refs
):
    transform, shift = transform_ref[...], shift_ref[...]
    write_products(
        slots, members, runners, plan, 1, transform, shift, own_ref, place_ref, table_ref, refs
    )


def own_means_of(slots, members, table_ref, seen_refs, cells):
    share = seen_refs[0].shape[1]
    own_means, mean = [], 0.0
    for step, ref in enumerate(seen_refs):
        packed = ref[slots:, :]
        row = jnp.concatenate(
            [joined(packed, 3 + 3 * index) for index in range(cells // share)], axis=1
        )
        own_means.append(row)
        mean = mean + row * count_row(table_ref, step, cells)
    return own_means, mean * (1.0 / members)


def write_products(
    slots, members, runners, plan, side, transform, shift, own_ref, place_ref, table_ref, refs
):
    seen_refs, refs = refs[:runners], refs[runners:]
    cell_refs, out_refs = refs[: -len(plan)], refs[-len(plan) :]
    width = out_refs[0].shape[1]
    own_means, mean = own_means_of(slots, members, table_ref, seen_refs, width * PARTS)
    rows = jnp.dot(own_ref[side], transform, preferred_element_type=F32).astype(BF16)
    both = jnp.concatenate([rows, shift], axis=0)
    lefts, sums = {}, {}
    for step in sorted({step for _, steps in plan for step in steps}):
        table = place_ref[:, step * slots : (step + 1) * slots]
        lefts[step] = jnp.dot(both, table, preferred_element_type=F32).astype(BF16)
        sums[step] = jnp.sum(lefts[step].astype(F32), axis=1, keepdims=True)
    place = 0
    for (part, steps), out_ref in zip(plan, out_refs):
        span = slice(part * width, (part + 1) * width)
        total = 0.0
        for step in steps:
            total = total + jnp.dot(
                lefts[step], cell_refs[place][...], preferred_element_type=F32
            )
            total = total + sums[step] * (own_means[step] - mean)[:, span]
            place = place + 1
        shift = joined(total[slots:], 0)
        if side:
            shift = shift + mean[:, span]
        out_ref[...] = (total[:slots] + shift).astype(out_ref.dtype)


def final_kernel(slots, rows, table_ref, *refs):
    own_refs, refs = refs[:PARTS], refs[PARTS:]
    other_refs, (out_hbm, out_ref, sems) = refs[:-3], refs[-3:]
    columns = out_ref.shape[1]
    count = count_row(table_ref, 0, columns)
    chunk = slots // WRITES
    copies = []
    for index in range(WRITES):
        start = index * chunk
        slot = lax.broadcasted_iota(jnp.int32, (chunk, columns), 0) + start
        live = slot.astype(F32) < count
        row = 0
        for part, own_ref in enumerate(own_refs):
            for first in range(0, own_ref.shape[1], columns):
                span = slice(first, first + columns)
                total = own_ref[start : start + chunk, span]
                if part >= GATHERED:
                    other = other_refs[part - GATHERED][start : start + chunk, span]
                    total = total + other.astype(F32)
                out_ref[pl.ds(start * rows + row, chunk, stride=rows), :] = jnp.where(
                    live, total, 0.0
                )
                row = row + 1
        span = pl.ds(start * rows, chunk * rows)
        copies.append(
            pltpu.make_async_copy(out_ref.at[span], out_hbm.at[span], sems.at[index])
        )
        copies[-1].start()
    for copy in copies:
        copy.wait()


def body(states, diffusivity, velocity, counts, obs_index, obs_value, obs_weight):
    runners = lax.axis_size("runner")
    blocks = lax.axis_size("cells")
    slots, rows, columns = states.shape
    members = slots // 2 * runners
    half = members // 2
    cells = rows * columns
    seen = obs_index.shape[0]
    shares = 2
    share = seen // shares
    height = slots + PAD
    shape = jax.ShapeDtypeStruct

    rank = lax.axis_index("runner").astype(jnp.int32).reshape(1)
    last, first, flat, fields = call(
        functools.partial(edge_kernel, slots, rows),
        [shape((STEPS, height, columns), BF16)] * 2
        + [shape((slots * rows, columns), F32), shape((3, rows, columns), F32)],
        [],
        [states.reshape(slots * rows, columns), diffusivity, velocity],
        [pltpu.SemaphoreType.DMA((3,))],
        outside=True,
    )
    forward = [(i, (i + 1) % blocks) for i in range(blocks)]
    backward = [(target, source) for source, target in forward]
    low = lax.ppermute(last, "cells", forward)
    high = lax.ppermute(first, "cells", backward)
    pick, both, place, own, table = call(
        functools.partial(setup_kernel, slots, runners, members, shares),
        [
            shape((cells, seen), BF16),
            shape((8, share), F32),
            shape((members, runners * slots), BF16),
            shape((2, slots, members), BF16),
            shape((runners, columns), F32),
        ],
        [counts, rank],
        [obs_index[None, :], obs_value[None, :], obs_weight[None, :]],
    )

    coefs, inner = call(
        functools.partial(inner_kernel, slots, rows),
        [
            shape((rows, 5, 8, columns), F32),
            shape((sum(len(inside) for inside in inner_rows(rows)), slots, columns), F32),
        ],
        [],
        [flat, fields],
    )
    lower = -(-(3 + 3 * (cells // share)) // PAD) * PAD
    kept, given, *own_cells = call(
        functools.partial(forecast_kernel, slots, rows, shares),
        [shape((slots + lower, share), BF16)] * shares
        + [shape((slots, cells // PARTS), BF16)] * PARTS,
        [],
        [table, flat, low, high, coefs, inner, pick],
        [
            pltpu.VMEM((rows + 2 * STEPS, 5, 8, columns), F32),
            pltpu.VMEM((rows, slots, columns), F32),
            pltpu.VMEM((height, cells), BF16),
        ],
    )

    def moved(array, runner_bit, block_bit=0):
        count = runners * blocks
        step = runner_bit * blocks + block_bit
        return lax.ppermute(array, ("runner", "cells"), partners(count, step))

    all_seen = [kept] + [
        moved(given if step % shares else kept, step)
        for step in range(1, runners)
    ]
    all_cells = {0: own_cells}
    bit = runners // 2
    while bit > 1:
        for step in list(all_cells):
            all_cells[step + bit] = [moved(array, bit) for array in all_cells[step]]
        bit = bit // 2
    even = sorted(all_cells)
    for part in range(GATHERED):
        for step in even:
            all_cells.setdefault(step + 1, []).append(moved(all_cells[step][part], 1))

    part = call(
        functools.partial(gram_kernel, slots, runners, members),
        shape((half + PAD, members), BF16),
        [],
        [*all_seen, table, both, place],
    )
    stages = [[(0, 1)], [(1, 0)]]
    width = 2
    while width < blocks:
        reach = min(4, blocks // width)
        stages.append([(0, width * step) for step in reversed(range(1, reach))])
        width = width * reach
    for index, stage in enumerate(stages):
        parts = [part] + [moved(part, r, c) for r, c in stage]
        if index + 1 < len(stages):
            part = call(
                functools.partial(sum_kernel, half),
                shape((half + PAD, members), BF16),
                [],
                parts,
            )

    def held(plan):
        return all_seen + [all_cells[step][part] for part, steps in plan for step in steps]

    shared = [(part, even) for part in range(GATHERED, PARTS)]
    *given_products, transform, shift = call(
        functools.partial(transform_kernel, slots, members, runners, len(parts), shared),
        [shape((slots, cells // PARTS), BF16)] * len(shared)
        + [shape((members, members), BF16), shape((PAD, members), BF16)],
        [],
        [*parts, place, own, table, *held(shared)],
    )
    other_products = [moved(array, 1) for array in given_products]
    plan = [(part, sorted(all_cells)) for part in range(GATHERED)] + shared
    own_products = call(
        functools.partial(keep_kernel, slots, members, runners, plan),
        [shape((slots, cells // PARTS), F32)] * len(plan),
        [],
        [transform, shift, own, place, table, *held(plan)],
    )
    analysed = call(
        functools.partial(final_kernel, slots, rows),
        shape((slots * rows, columns), F32),
        [],
        [table, *own_products, *other_products],
        [pltpu.VMEM((slots * rows, columns), F32), pltpu.SemaphoreType.DMA((WRITES,))],
        write=True,
    )
    return analysed.reshape(slots, rows, columns)


def solution(mesh):
    return jax.shard_map(
        body,
        mesh=mesh,
        in_specs=(
            P("runner", "cells", None),
            P("cells", None),
            P(None, "cells", None),
            P(),
            P("cells"),
            P("cells"),
            P("cells"),
        ),
        out_specs=P("runner", "cells", None),
        check_vma=False,
    )
```

```python
import functools

import jax
import jax.numpy as jnp
from jax import lax
from jax.experimental import pallas as pl
from jax.experimental.pallas import tpu as pltpu
from jax.sharding import PartitionSpec as P


STEPS = 4
PAD = 16
F32 = jnp.float32
BF16 = jnp.bfloat16

PARTS = 2
WRITES = 4
GATHERED = 1


def partners(count, step):
    return [(i, i ^ step) for i in range(count)]


def pieces(row):
    high = row.astype(BF16).astype(F32)
    rest = row - high
    middle = rest.astype(BF16).astype(F32)
    return high, middle, rest - middle


def stacked(rows, height, dtype=BF16):
    width = rows[0].shape[1]
    place = lax.broadcasted_iota(jnp.int32, (height, width), 0)
    total = jnp.zeros((height, width), F32)
    for index, row in enumerate(rows):
        total = jnp.where(place == index, row, total)
    return total.astype(dtype)


def joined(block, first):
    block = block.astype(F32)
    return block[first : first + 1] + block[first + 1 : first + 2] + block[first + 2 : first + 3]


def offset_of(counts_ref, runner, runners):
    total = jnp.int32(0)
    for index in range(runners):
        total = total + jnp.where(index < runner, counts_ref[index], 0)
    return total


def count_row(table_ref, step, width):
    return jnp.tile(table_ref[step : step + 1, :], (1, width // table_ref.shape[1]))


def size_of(shape):
    size = shape.dtype.itemsize
    for extent in shape.shape:
        size = size * extent
    return size


def call(kernel, out_shape, scalars, vectors, scratch=(), outside=False, write=False):
    vector = pl.BlockSpec(memory_space=pltpu.VMEM)
    scalar = pl.BlockSpec(memory_space=pltpu.SMEM)
    hbm = pl.BlockSpec(memory_space=pltpu.HBM)
    if outside:
        vectors = [pltpu.with_memory_space_constraint(array, pltpu.HBM) for array in vectors]
    many = isinstance(out_shape, list)
    shapes = list(vectors) + (out_shape if many else [out_shape])
    held = sum(size_of(shape) for shape in shapes)
    return pl.pallas_call(
        kernel,
        out_shape=out_shape,
        in_specs=[scalar] * len(scalars) + [hbm if outside else vector] * len(vectors),
        out_specs=hbm if write else [vector] * len(out_shape) if many else vector,
        scratch_shapes=list(scratch),
        compiler_params=pltpu.CompilerParams(
            vmem_limit_bytes=min(56 << 20, (12 << 20) + 3 * held)
        ),
        cost_estimate=pl.CostEstimate(flops=0, bytes_accessed=1 << 20, transcendentals=0),
    )(*scalars, *vectors)


def edge_kernel(
    slots, rows, states_hbm, diff_hbm, vel_hbm, last_ref, first_ref, states_ref, fields_ref, sems
):
    copies = [
        pltpu.make_async_copy(states_hbm, states_ref, sems.at[0]),
        pltpu.make_async_copy(diff_hbm, fields_ref.at[0], sems.at[1]),
        pltpu.make_async_copy(vel_hbm, fields_ref.at[pl.ds(1, 2)], sems.at[2]),
    ]
    for copy in copies:
        copy.start()
    for copy in copies:
        copy.wait()
    for out_ref, base in ((last_ref, rows - STEPS), (first_ref, 0)):
        for j in range(STEPS):
            row = base + j
            out_ref[j, :slots, :] = states_ref[pl.ds(row, slots, stride=rows), :].astype(BF16)
            packed = []
            for field in range(3):
                packed.extend(pieces(fields_ref[field, row : row + 1]))
            out_ref[j, slots:, :] = stacked(packed, PAD)


def coefficients(diff, along, across):
    columns = diff.shape[1]
    return [
        jnp.broadcast_to(coef, (8, columns))
        for coef in (
            1.0 - 4.0 * diff,
            diff - 0.5 * along,
            diff + 0.5 * along,
            diff - 0.5 * across,
            diff + 0.5 * across,
        )
    ]


def advanced(u, above, below, coefs):
    columns = u.shape[1]
    return (
        u * (coefs[0] - 0.05 * (u * u))
        + coefs[1] * above
        + coefs[2] * below
        + coefs[3] * pltpu.roll(u, columns - 1, 1)
        + coefs[4] * pltpu.roll(u, 1, 1)
    )


def inner_rows(rows):
    return [range(step, rows - step) for step in range(1, STEPS) if step < rows - step]


def inner_kernel(slots, rows, states_ref, fields_ref, coef_ref, inner_ref):
    for row in range(rows):
        fields = [fields_ref[field, row : row + 1] for field in range(3)]
        for index, coef in enumerate(coefficients(*fields)):
            coef_ref[row, index] = coef
    for start in range(0, slots, 16):
        values = []
        for row in range(rows):
            block = states_ref[pl.ds(start * rows + row, 16, stride=rows), :]
            values.append([block[8 * h : 8 * h + 8] for h in range(2)])
        place = 0
        for inside in inner_rows(rows):
            after = list(values)
            for row in inside:
                coefs = [coef_ref[row, index] for index in range(5)]
                after[row] = [
                    advanced(values[row][h], values[row + 1][h], values[row - 1][h], coefs)
                    for h in range(2)
                ]
                for h in range(2):
                    inner_ref[place, start + 8 * h : start + 8 * h + 8, :] = after[row][h]
                place = place + 1
            values = after


def forecast_kernel(
    slots, rows, shares, table_ref, states_ref, low_ref, high_ref, own_coef_ref, inner_ref,
    pick_ref, *rest,
):
    (coef_ref, value_ref, cells_ref) = rest[-3:]
    seen_refs, mean_ref, part_refs = rest[: shares - 1], rest[shares - 1], rest[shares:-3]
    columns = states_ref.shape[1]
    total_rows = rows + 2 * STEPS
    count = count_row(table_ref, 0, columns)

    for row in [*range(1, STEPS), *range(STEPS + rows, total_rows - 1)]:
        block = (low_ref[row] if row < STEPS else high_ref[row - STEPS - rows])[slots:]
        fields = [joined(block, 3 * field) for field in range(3)]
        for index, coef in enumerate(coefficients(*fields)):
            coef_ref[row, index] = coef

    known = {}
    for step, inside in enumerate(inner_rows(rows)):
        for row in inside:
            known[step, row + STEPS] = len(known)
    chunk = 16
    halves = chunk // 8
    sums = [jnp.zeros((8, columns), F32)] * rows
    for start in range(0, slots, chunk):
        values = []
        for row in range(total_rows):
            if row < STEPS:
                block = low_ref[row, start : start + chunk, :].astype(F32)
            elif row < STEPS + rows:
                block = states_ref[pl.ds(start * rows + row - STEPS, chunk, stride=rows), :]
            else:
                block = high_ref[row - STEPS - rows, start : start + chunk, :].astype(F32)
            values.append([block[8 * h : 8 * h + 8] for h in range(halves)])
        for step in range(STEPS):
            after = list(values)
            for row in range(step + 1, total_rows - step - 1):
                if (step, row) in known:
                    block = inner_ref[known[step, row], start : start + chunk, :]
                    after[row] = [block[8 * h : 8 * h + 8] for h in range(halves)]
                    continue
                if STEPS <= row < STEPS + rows:
                    coefs = [own_coef_ref[row - STEPS, index] for index in range(5)]
                else:
                    coefs = [coef_ref[row, index] for index in range(5)]
                after[row] = [
                    advanced(values[row][h], values[row + 1][h], values[row - 1][h], coefs)
                    for h in range(halves)
                ]
            values = after
        for h in range(halves):
            place = lax.broadcasted_iota(jnp.int32, (8, columns), 0) + (start + 8 * h)
            live = place.astype(F32) < count
            for row in range(rows):
                u = jnp.where(live, values[row + STEPS][h], 0.0)
                sums[row] = sums[row] + u
                value_ref[row, start + 8 * h : start + 8 * h + 8, :] = u

    live = lax.broadcasted_iota(jnp.int32, (slots, columns), 0).astype(F32) < count
    inverse = 1.0 / count
    means = []
    for row in range(rows):
        mean = jnp.sum(sums[row], axis=0, keepdims=True) * inverse
        part = jnp.where(live, value_ref[row] - mean, 0.0).astype(BF16)
        cells_ref[:slots, row * columns : (row + 1) * columns] = part
        cells_ref[slots:, row * columns : (row + 1) * columns] = stacked(pieces(mean), PAD)
        means.append(mean)
    width = rows * columns // len(part_refs)
    for index, part_ref in enumerate(part_refs):
        part_ref[...] = cells_ref[:slots, index * width : (index + 1) * width]
    mean_ref[...] = cells_ref[slots:, :]
    share = pick_ref.shape[1] // shares
    seen = jnp.dot(cells_ref[...], pick_ref[:, share:], preferred_element_type=F32)
    packed = [jnp.zeros((1, share), F32)] * 3
    for first in range(0, rows, share // columns):
        packed.extend(
            pieces(jnp.concatenate(means[first : first + share // columns], axis=1))
        )
    packed = stacked(packed, seen_refs[0].shape[0] - slots)
    for index, seen_ref in enumerate(seen_refs):
        part = seen[:, index * share : (index + 1) * share].astype(BF16)
        seen_ref[:slots, :] = part[:slots]
        seen_ref[slots : slots + PAD, :] = part[slots:] + packed[:PAD]
        if packed.shape[0] > PAD:
            seen_ref[slots + PAD :, :] = packed[PAD:]


def kept_kernel(slots, mean_ref, given_ref, pick_ref, *refs):
    part_refs, out_ref = refs[:-1], refs[-1]
    share = out_ref.shape[1]
    width = part_refs[0].shape[1]
    total = 0.0
    for index, ref in enumerate(part_refs):
        rows = slice(index * width, (index + 1) * width)
        total = total + jnp.dot(ref[...], pick_ref[rows, :share], preferred_element_type=F32)
    means = jnp.dot(mean_ref[...], pick_ref[:, :share], preferred_element_type=F32)
    lower = given_ref[slots : slots + PAD, :].astype(F32)
    place = lax.broadcasted_iota(jnp.int32, lower.shape, 0)
    out_ref[:slots, :] = total.astype(BF16)
    out_ref[slots : slots + PAD, :] = jnp.where(place < 3, means, lower).astype(BF16)
    if out_ref.shape[0] > slots + PAD:
        out_ref[slots + PAD :, :] = given_ref[slots + PAD :, :]


def placing(slots, runners, members, counts_ref, runner, by_slot):
    shape, slot_dim = ((slots, members), 0) if by_slot else ((members, slots), 1)
    slot = lax.broadcasted_iota(jnp.int32, shape, slot_dim)
    member = lax.broadcasted_iota(jnp.int32, shape, 1 - slot_dim)
    offset = offset_of(counts_ref, runner, runners)
    hit = (member - slot == offset) & (slot < counts_ref[runner])
    return jnp.where(hit, 1.0, 0.0).astype(BF16)


def setup_kernel(
    slots, runners, members, shares, counts_ref, rank_ref, index_ref, value_ref, weight_ref,
    pick_ref, seen_ref, place_ref, own_ref, table_ref,
):
    rank = rank_ref[0]
    share = index_ref.shape[1] // shares

    def own_first(ref):
        swapped = jnp.concatenate([ref[:, share:], ref[:, :share]], axis=1)
        return jnp.where(jnp.bitwise_and(rank, 1) == 0, ref[...], swapped)

    wanted = own_first(index_ref)
    cell = lax.broadcasted_iota(jnp.int32, pick_ref.shape, 0)
    pick_ref[...] = jnp.where(cell == wanted, 1.0, 0.0).astype(BF16)
    seen_ref[...] = stacked([own_first(value_ref)[:, :share], own_first(weight_ref)[:, :share]], 8, F32)
    for step in range(runners):
        place_ref[:, step * slots : (step + 1) * slots] = placing(
            slots, runners, members, counts_ref, rank ^ step, False
        )
        count = jnp.full((1, table_ref.shape[1]), counts_ref[rank ^ step], jnp.int32)
        table_ref[step : step + 1, :] = count.astype(F32)
    for side in range(2):
        own_ref[side] = placing(slots, runners, members, counts_ref, rank ^ (1 - side), True)


def triangles(members):
    half = members // 2
    row = lax.broadcasted_iota(jnp.int32, (half, half), 0)
    column = lax.broadcasted_iota(jnp.int32, (half, half), 1)
    return half, row, column


def gram_kernel(slots, runners, members, *refs):
    seen_refs, (table_ref, both_ref, place_ref, out_ref) = refs[:runners], refs[runners:]
    own_means = [joined(ref[slots:, :], 0) for ref in seen_refs]
    width = both_ref.shape[1]
    mean = 0.0
    for step, row in enumerate(own_means):
        mean = mean + row * count_row(table_ref, step, width)
    mean = mean * (1.0 / members)
    observed = 0.0
    for step, ref in enumerate(seen_refs):
        part = ref[:slots, :].astype(F32) + (own_means[step] - mean)
        place = place_ref[:, step * slots : (step + 1) * slots]
        observed = observed + jnp.dot(place, part.astype(BF16), preferred_element_type=F32)
    weighted = (observed * both_ref[1:2, :]).astype(BF16)
    across = (((1,), (1,)), ((), ()))
    gram = lax.dot_general(
        weighted, observed.astype(BF16), across, preferred_element_type=F32
    )
    innovation = stacked(pieces(both_ref[0:1, :] - mean), PAD)
    bias = lax.dot_general(innovation, weighted, across, preferred_element_type=F32)
    half, row, column = triangles(members)
    last = gram[half:, half:]
    out_ref[:half, :half] = jnp.where(row >= column, gram[:half, :half], last).astype(BF16)
    out_ref[:half, half:] = gram[:half, half:].astype(BF16)
    diagonal = jnp.sum(jnp.where(row == column, last, 0.0), axis=0, keepdims=True)
    diagonal = jnp.concatenate([diagonal, jnp.zeros_like(diagonal)], axis=1)
    out_ref[half:, :] = stacked([*pieces(joined(bias, 0)), *pieces(diagonal)], PAD)


def total_of(half, part_refs):
    packed, bias, diagonal = 0.0, 0.0, 0.0
    for ref in part_refs:
        packed = packed + ref[:half, :].astype(F32)
        bias = bias + joined(ref[half:, :], 0)
        diagonal = diagonal + joined(ref[half:, :], 3)
    return packed, bias, diagonal


def sum_kernel(half, *refs):
    part_refs, out_ref = refs[:-1], refs[-1]
    packed, bias, diagonal = total_of(half, part_refs)
    out_ref[:half, :] = packed.astype(BF16)
    out_ref[half:, :] = stacked([*pieces(bias), *pieces(diagonal)], PAD)


def transform_kernel(slots, members, runners, sums, plan, *refs):
    part_refs, refs = refs[:sums], refs[sums:]
    (place_ref, own_ref, table_ref), refs = refs[:3], refs[3:]
    (transform_ref, shift_ref), refs = refs[-2:], refs[:-2]
    half, row, column = triangles(members)
    packed, bias, diagonal = total_of(half, part_refs)
    corner, side = packed[:, :half], packed[:, half:]
    mirror = jnp.transpose(corner)
    first = jnp.where(row >= column, corner, mirror)
    last = jnp.where(
        row < column, corner, jnp.where(row == column, diagonal[:, :half], mirror)
    )
    gram = jnp.concatenate(
        [
            jnp.concatenate([first, side], axis=1),
            jnp.concatenate([jnp.transpose(side), last], axis=1),
        ],
        axis=0,
    )
    trace = jnp.sum(
        jnp.sum(jnp.where(row == column, first + last, 0.0), axis=0, keepdims=True),
        axis=1, keepdims=True,
    )
    scaling = float(members) / trace
    scaled = (gram * scaling).astype(BF16)
    bias = (bias * scaling).astype(BF16).astype(F32)

    def times(left):
        return jnp.dot(left, scaled, preferred_element_type=F32)

    first_power = times(jnp.concatenate([scaled, stacked([bias], PAD)], axis=0))
    square = first_power[:members].astype(BF16)
    bias_1 = first_power[members : members + 1]
    second_power = times(jnp.concatenate([square, stacked(pieces(bias_1), PAD)], axis=0))
    cubed = second_power[:members]
    bias_2 = joined(second_power[members:], 0)
    bias_3 = joined(times(stacked(pieces(bias_2), PAD)), 0)
    shift = bias - 0.5 * bias_1 + 0.375 * bias_2 - 0.3125 * bias_3
    identity = lax.broadcasted_iota(jnp.int32, (members, members), 0) == (
        lax.broadcasted_iota(jnp.int32, (members, members), 1)
    )
    transform = (
        jnp.where(identity, 1.0, 0.0)
        - 0.5 * scaled.astype(F32)
        + 0.375 * square.astype(F32)
        - 0.3125 * cubed
    ).astype(BF16)
    shift = stacked(pieces(shift), PAD)
    transform_ref[...] = transform
    shift_ref[...] = shift
    write_products(
        slots, members, runners, plan, 0, transform, shift, own_ref, place_ref, table_ref, refs
    )


def keep_kernel(
    slots, members, runners, plan, transform_ref, shift_ref, own_ref, place_ref, table_ref, *refs
):
    transform, shift = transform_ref[...], shift_ref[...]
    write_products(
        slots, members, runners, plan, 1, transform, shift, own_ref, place_ref, table_ref, refs
    )


def own_means_of(slots, members, table_ref, seen_refs, cells):
    share = seen_refs[0].shape[1]
    own_means, mean = [], 0.0
    for step, ref in enumerate(seen_refs):
        packed = ref[slots:, :]
        row = jnp.concatenate(
            [joined(packed, 3 + 3 * index) for index in range(cells // share)], axis=1
        )
        own_means.append(row)
        mean = mean + row * count_row(table_ref, step, cells)
    return own_means, mean * (1.0 / members)


def write_products(
    slots, members, runners, plan, side, transform, shift, own_ref, place_ref, table_ref, refs
):
    seen_refs, refs = refs[:runners], refs[runners:]
    cell_refs, out_refs = refs[: -len(plan)], refs[-len(plan) :]
    width = out_refs[0].shape[1]
    own_means, mean = own_means_of(slots, members, table_ref, seen_refs, width * PARTS)
    rows = jnp.dot(own_ref[side], transform, preferred_element_type=F32).astype(BF16)
    both = jnp.concatenate([rows, shift], axis=0)
    lefts, sums = {}, {}
    for step in sorted({step for _, steps in plan for step in steps}):
        table = place_ref[:, step * slots : (step + 1) * slots]
        lefts[step] = jnp.dot(both, table, preferred_element_type=F32).astype(BF16)
        sums[step] = jnp.sum(lefts[step].astype(F32), axis=1, keepdims=True)
    place = 0
    for (part, steps), out_ref in zip(plan, out_refs):
        span = slice(part * width, (part + 1) * width)
        total = 0.0
        for step in steps:
            total = total + jnp.dot(
                lefts[step], cell_refs[place][...], preferred_element_type=F32
            )
            total = total + sums[step] * (own_means[step] - mean)[:, span]
            place = place + 1
        shift = joined(total[slots:], 0)
        if side:
            shift = shift + mean[:, span]
        out_ref[...] = (total[:slots] + shift).astype(out_ref.dtype)


def final_kernel(slots, rows, table_ref, *refs):
    own_refs, refs = refs[:PARTS], refs[PARTS:]
    other_refs, (out_hbm, out_ref, sems) = refs[:-3], refs[-3:]
    columns = out_ref.shape[1]
    count = count_row(table_ref, 0, columns)
    chunk = slots // WRITES
    copies = []
    for index in range(WRITES):
        start = index * chunk
        slot = lax.broadcasted_iota(jnp.int32, (chunk, columns), 0) + start
        live = slot.astype(F32) < count
        row = 0
        for part, own_ref in enumerate(own_refs):
            for first in range(0, own_ref.shape[1], columns):
                span = slice(first, first + columns)
                total = own_ref[start : start + chunk, span]
                if part >= GATHERED:
                    other = other_refs[part - GATHERED][start : start + chunk, span]
                    total = total + other.astype(F32)
                out_ref[pl.ds(start * rows + row, chunk, stride=rows), :] = jnp.where(
                    live, total, 0.0
                )
                row = row + 1
        span = pl.ds(start * rows, chunk * rows)
        copies.append(
            pltpu.make_async_copy(out_ref.at[span], out_hbm.at[span], sems.at[index])
        )
        copies[-1].start()
    for copy in copies:
        copy.wait()


def body(states, diffusivity, velocity, counts, obs_index, obs_value, obs_weight):
    runners = lax.axis_size("runner")
    blocks = lax.axis_size("cells")
    slots, rows, columns = states.shape
    members = slots // 2 * runners
    half = members // 2
    cells = rows * columns
    seen = obs_index.shape[0]
    shares = 2
    share = seen // shares
    height = slots + PAD
    shape = jax.ShapeDtypeStruct

    rank = lax.axis_index("runner").astype(jnp.int32).reshape(1)
    last, first, flat, fields = call(
        functools.partial(edge_kernel, slots, rows),
        [shape((STEPS, height, columns), BF16)] * 2
        + [shape((slots * rows, columns), F32), shape((3, rows, columns), F32)],
        [],
        [states.reshape(slots * rows, columns), diffusivity, velocity],
        [pltpu.SemaphoreType.DMA((3,))],
        outside=True,
    )
    forward = [(i, (i + 1) % blocks) for i in range(blocks)]
    backward = [(target, source) for source, target in forward]
    low = lax.ppermute(last, "cells", forward)
    high = lax.ppermute(first, "cells", backward)
    pick, both, place, own, table = call(
        functools.partial(setup_kernel, slots, runners, members, shares),
        [
            shape((cells, seen), BF16),
            shape((8, share), F32),
            shape((members, runners * slots), BF16),
            shape((2, slots, members), BF16),
            shape((runners, columns), F32),
        ],
        [counts, rank],
        [obs_index[None, :], obs_value[None, :], obs_weight[None, :]],
    )

    coefs, inner = call(
        functools.partial(inner_kernel, slots, rows),
        [
            shape((rows, 5, 8, columns), F32),
            shape((sum(len(inside) for inside in inner_rows(rows)), slots, columns), F32),
        ],
        [],
        [flat, fields],
    )
    lower = -(-(3 + 3 * (cells // share)) // PAD) * PAD
    given, own_mean, *own_cells = call(
        functools.partial(forecast_kernel, slots, rows, shares),
        [shape((slots + lower, share), BF16), shape((PAD, cells), BF16)]
        + [shape((slots, cells // PARTS), BF16)] * PARTS,
        [],
        [table, flat, low, high, coefs, inner, pick],
        [
            pltpu.VMEM((rows + 2 * STEPS, 5, 8, columns), F32),
            pltpu.VMEM((rows, slots, columns), F32),
            pltpu.VMEM((height, cells), BF16),
        ],
    )

    kept = call(
        functools.partial(kept_kernel, slots),
        shape((slots + lower, share), BF16),
        [],
        [own_mean, given, pick, *own_cells],
    )

    def moved(array, runner_bit, block_bit=0):
        count = runners * blocks
        step = runner_bit * blocks + block_bit
        return lax.ppermute(array, ("runner", "cells"), partners(count, step))

    all_seen = [kept] + [
        moved(given if step % shares else kept, step)
        for step in range(1, runners)
    ]
    all_cells = {0: own_cells}
    bit = runners // 2
    while bit > 1:
        for step in list(all_cells):
            all_cells[step + bit] = [moved(array, bit) for array in all_cells[step]]
        bit = bit // 2
    even = sorted(all_cells)
    for part in range(GATHERED):
        for step in even:
            all_cells.setdefault(step + 1, []).append(moved(all_cells[step][part], 1))

    part = call(
        functools.partial(gram_kernel, slots, runners, members),
        shape((half + PAD, members), BF16),
        [],
        [*all_seen, table, both, place],
    )
    stages = [[(0, 1)], [(1, 0)]]
    width = 2
    while width < blocks:
        reach = min(4, blocks // width)
        stages.append([(0, width * step) for step in reversed(range(1, reach))])
        width = width * reach
    for index, stage in enumerate(stages):
        parts = [part] + [moved(part, r, c) for r, c in stage]
        if index + 1 < len(stages):
            part = call(
                functools.partial(sum_kernel, half),
                shape((half + PAD, members), BF16),
                [],
                parts,
            )

    def held(plan):
        return all_seen + [all_cells[step][part] for part, steps in plan for step in steps]

    shared = [(part, even) for part in range(GATHERED, PARTS)]
    *given_products, transform, shift = call(
        functools.partial(transform_kernel, slots, members, runners, len(parts), shared),
        [shape((slots, cells // PARTS), BF16)] * len(shared)
        + [shape((members, members), BF16), shape((PAD, members), BF16)],
        [],
        [*parts, place, own, table, *held(shared)],
    )
    other_products = [moved(array, 1) for array in given_products]
    plan = [(part, sorted(all_cells)) for part in range(GATHERED)] + shared
    own_products = call(
        functools.partial(keep_kernel, slots, members, runners, plan),
        [shape((slots, cells // PARTS), F32)] * len(plan),
        [],
        [transform, shift, own, place, table, *held(plan)],
    )
    analysed = call(
        functools.partial(final_kernel, slots, rows),
        shape((slots * rows, columns), F32),
        [],
        [table, *own_products, *other_products],
        [pltpu.VMEM((slots * rows, columns), F32), pltpu.SemaphoreType.DMA((WRITES,))],
        write=True,
    )
    return analysed.reshape(slots, rows, columns)


def solution(mesh):
    return jax.shard_map(
        body,
        mesh=mesh,
        in_specs=(
            P("runner", "cells", None),
            P("cells", None),
            P(None, "cells", None),
            P(),
            P("cells"),
            P("cells"),
            P("cells"),
        ),
        out_specs=P("runner", "cells", None),
        check_vma=False,
    )
```
